32 devices in a mesh: groups: 2 (over x), gx: 16 (over z, y, core), gy: 1.
Axes of the slice: x: 2, y: 2, z: 4, core: 2. Of those that a mesh axis runs over, the one named last changes fastest.
Arguments:
- field: float32 [64, 32, 2048], P(('groups', 'gx'), 'gy'), parts along dimension 0, may hold values from -6 to 6
- spectral: float32 [32, 32, 16, 2, 32, 32], P('gy', 'gx'), may hold values from -2.1213202 to 2.1213202
- conv_first: float32 [3, 3, 3, 32, 32], replicated, may hold values from -0.21875 to 0.21875
- conv_second: float32 [3, 3, 3, 32, 32], replicated, may hold values from -0.21875 to 0.21875
- bias: float32 [32], replicated, may hold values from -3 to 3
Outputs:
- block_output: float32 [64, 32, 2048], P(('groups', 'gx'), 'gy'), parts along dimension 0
The draws below stay inside these ranges and needn't reach their ends.
There are 2 independent parts, one for each index of `groups`. The reference program is written for one: setup_inputs(seed, part) draws one part's arguments, and reference() takes and returns one part's arrays. A program takes and returns all parts, laid end to end along the dimension named above; an argument that names none is the same for every part. Nothing has to cross between parts.
All inputs are finite; a program needn't handle non-finite values.
Results may differ from the reference program's by a relative error of at most 0.000057.
Values sent between devices are 32-bit elements; how exact they have to be, the bound alone decides.
A program may use at most 128 MiB of HBM per device.

```python
import jax
import jax.numpy as jnp
from jax import lax

CH = 32
NZ = 64
MX = 32
MY = 32
MZ = 16
NX = 32
NY = 32


def shard_levels(stream_key, dims, cuts, smallest, top_value):
    def one(position, parts):
        steps = jax.random.uniform(jax.random.fold_in(jax.random.fold_in(stream_key, 6), position), (parts,), jnp.float32, smallest / len(cuts), top_value / len(cuts))
        return jnp.repeat(jnp.exp(steps), dims[position] // parts).reshape((-1,) + (1,) * (len(dims) - position - 1))

    gain = one(*cuts[0])
    for cut in cuts[1:]:
        gain = gain * one(*cut)
    return gain


def gaussian(stream_key, extent, scale, reach, split=(), kind=jnp.bfloat16):
    drawn = jax.random.normal(stream_key, extent, jnp.float32) * scale
    if len(split) > 0:
        drawn = shard_levels(stream_key, extent, split, -0.22, 0.18) * drawn
    return jnp.clip(drawn, min=-reach, max=reach).astype(kind)


def setup_inputs(seed: int = 0, part: int = 0) -> dict:
    seeds = jax.random.split(jax.random.key(seed), 6)
    part_splits = jax.random.split(jax.random.fold_in(seeds[5], part), 6)
    field = gaussian(part_splits[0], (NX, NY, NZ * CH), 1.0, 6.0, ((0, 16),), jnp.float32)
    spectral = gaussian(seeds[1], (MY, MX, MZ, 2, CH, CH), (2 / CH ** 0.5), 2.1213202, ((1, 16),), jnp.float32)
    conv_first = gaussian(seeds[2], (3, 3, 3, CH, CH), (27 * CH) ** -0.5, 0.21875, (), jnp.float32)
    conv_second = gaussian(seeds[3], (3, 3, 3, CH, CH), (27 * CH) ** -0.5, 0.21875, (), jnp.float32)
    bias = gaussian(seeds[4], (CH,), 0.5, 3.0, (), jnp.float32)
    return dict(field=field, spectral=spectral, conv_first=conv_first, conv_second=conv_second, bias=bias)


def positions(length, retained):
    counter = jnp.arange(retained, dtype=jnp.int32)
    return jnp.where(counter < retained // 2, counter, length - retained + counter)


def convolve(volume, weight):
    return lax.conv_general_dilated(volume[None], weight, (1, 1, 1), "SAME", dimension_numbers=("NDHWC", "DHWIO", "NDHWC"), precision=lax.Precision.HIGHEST)[0]


def reference(field, spectral, conv_first, conv_second, bias):
    volume = field.reshape(NX, NY, NZ, CH)
    spectrum = jnp.fft.rfftn(volume, axes=(0, 1, 2))
    rows_x = positions(NX, MX)
    rows_y = positions(NY, MY)
    retained_modes = spectrum[rows_x][:, rows_y][:, :, :MZ]
    matrix = spectral[:, :, :, 0] + 1j * spectral[:, :, :, 1]
    mixed = jnp.einsum("abzi,bazio->abzo", retained_modes, matrix, precision=lax.Precision.HIGHEST)
    full_spectrum = jnp.zeros(spectrum.shape, spectrum.dtype).at[rows_x[:, None], rows_y[None, :], :MZ].set(mixed)
    spectral_part = jnp.fft.irfftn(full_spectrum, s=(NX, NY, NZ), axes=(0, 1, 2))
    first_hidden = jax.nn.gelu(convolve(volume, conv_first), approximate=False)
    second_branch = convolve(first_hidden, conv_second)
    result = jax.nn.gelu(spectral_part + second_branch + bias, approximate=False)
    return result.reshape(NX, NY, NZ * CH)
```

```python
import math

import jax
import jax.numpy as jnp
from jax import lax
from jax.experimental import pallas as pl
from jax.experimental.pallas import tpu as pltpu
from jax.sharding import PartitionSpec as P

CH = 32
NZ = 64
MX = 32
MY = 32
MZ = 16


HIGHEST = lax.Precision.HIGHEST
HIGH = lax.Precision.HIGH


def with_halo(cells, sides, width):
    for axis, dim in sides:
        count = lax.axis_size(axis)
        ends = count - 1
        head = lax.slice_in_dim(cells, 0, width, axis=dim)
        tail = lax.slice_in_dim(cells, cells.shape[dim] - width, cells.shape[dim], axis=dim)
        cells = jnp.concatenate(
            [
                lax.ppermute(tail, axis, [(i, (i + 1) % count) for i in range(ends)]),
                cells,
                lax.ppermute(head, axis, [((i + 1) % count, i) for i in range(ends)]),
            ],
            axis=dim,
        )
    return cells


def frequency(position, length, retained):
    return jnp.where(position < retained // 2, position, length - retained + position)


def angle_table(first_list, second_list, length):
    product = first_list[:, None] * second_list[None, :] % length
    angles = product.astype(jnp.float32) * (2.0 * math.pi / length)
    return (jnp.cos(angles), jnp.sin(angles))


def rotate_sum(cos_table, sin_table, values, pattern, direction_sign):
    real_part = values[:, :, 0]
    imag_part = values[:, :, 1]
    out_real = jnp.einsum(
        pattern, cos_table, real_part, precision=HIGHEST
    ) + direction_sign * jnp.einsum(pattern, sin_table, imag_part, precision=HIGHEST)
    out_imag = jnp.einsum(
        pattern, cos_table, imag_part, precision=HIGHEST
    ) - direction_sign * jnp.einsum(pattern, sin_table, real_part, precision=HIGHEST)
    return jnp.stack([out_real, out_imag], axis=2)


def convolve(padded, weight):
    extent_x = padded.shape[0] - 2
    extent_y = padded.shape[1] - 2
    volume = padded.reshape(padded.shape[0], padded.shape[1], NZ, CH)
    volume = jnp.pad(volume, ((0, 0), (0, 0), (1, 1), (0, 0)))
    kernel = weight.reshape(3, 3, 3 * CH, CH)

    def plane(start):
        slab = lax.dynamic_slice_in_dim(volume, start, 3, 0)
        accumulated = jnp.zeros((extent_y, NZ, CH), jnp.float32)
        for shift_x in range(3):
            for shift_y in range(3):
                windowed = slab[shift_x, shift_y : shift_y + extent_y]
                stacked = jnp.concatenate(
                    [windowed[:, shift_z : shift_z + NZ] for shift_z in range(3)], axis=2
                )
                accumulated = accumulated + jnp.einsum(
                    "yzi,io->yzo", stacked, kernel[shift_x, shift_y], precision=HIGHEST
                )
        return accumulated

    return lax.map(plane, jnp.arange(extent_x, dtype=jnp.int32))


def mode_mix(inputs, matrix):
    return jnp.einsum("bazi,bazio->bazo", inputs, matrix, precision=HIGHEST)


def body(field, spectral, conv_first, conv_second, bias):
    cells_x, cells_y, merged_width = field.shape
    devices_x = lax.axis_size("gx")
    devices_y = lax.axis_size("gy")
    extent_x = cells_x * devices_x
    extent_y = cells_y * devices_y
    owned_x = MX // devices_x
    owned_y = MY // devices_y
    y_places = lax.axis_index("gy") * cells_y + jnp.arange(cells_y, dtype=jnp.int32)
    mode_width = MZ * CH
    volume = field.reshape(cells_x, cells_y, NZ, CH)
    z_modes_index = jnp.arange(MZ, dtype=jnp.int32)
    z_cos, z_sin = angle_table(z_modes_index, jnp.arange(NZ, dtype=jnp.int32), NZ)
    z_real = jnp.einsum("xyzc,kz->xykc", volume, z_cos, precision=HIGHEST)
    z_imag = -jnp.einsum("xyzc,kz->xykc", volume, z_sin, precision=HIGHEST)
    z_spectrum = jnp.stack([z_real, z_imag], axis=2).reshape(cells_x, cells_y, 2, mode_width)
    cos_table, sin_table = angle_table(
        frequency(jnp.arange(MX, dtype=jnp.int32), extent_x, MX),
        jnp.arange(extent_x, dtype=jnp.int32),
        extent_x,
    )
    kept_modes = rotate_sum(
        cos_table,
        sin_table,
        lax.all_to_all(z_spectrum, "gx", split_axis=1, concat_axis=0, tiled=True),
        "kx,xym->kym",
        1.0,
    )
    x_modes = lax.all_to_all(kept_modes, "gx", split_axis=0, concat_axis=1, tiled=True)
    row_index = jnp.arange(owned_y * lax.axis_size("gy"), dtype=jnp.int32)
    cos_table, sin_table = angle_table(frequency(row_index, extent_y, MY), y_places, extent_y)
    all_modes = lax.psum_scatter(
        rotate_sum(cos_table, sin_table, x_modes, "ky,xym->kxm", 1.0),
        "gy",
        scatter_dimension=0,
        tiled=True,
    )
    complex_parts = all_modes.reshape(owned_y, owned_x, 2, MZ, CH)
    real_inputs = complex_parts[:, :, 0]
    imag_inputs = complex_parts[:, :, 1]
    weight_real = spectral[:, :, :, 0]
    weight_imag = spectral[:, :, :, 1]
    mixed_real = mode_mix(real_inputs, weight_real) - mode_mix(imag_inputs, weight_imag)
    mixed_imag = mode_mix(real_inputs, weight_imag) + mode_mix(imag_inputs, weight_real)
    mixed = jnp.stack([mixed_real, mixed_imag], axis=2).reshape(owned_y, owned_x, 2, mode_width)
    portion = lax.all_gather(mixed, "gy", axis=0, tiled=True)
    row_index = jnp.arange(portion.shape[0], dtype=jnp.int32)
    cos_table, sin_table = angle_table(y_places, frequency(row_index, extent_y, MY), extent_y)
    y_cells = rotate_sum(cos_table, sin_table, portion, "yk,kxm->xym", -1.0)
    cos_table, sin_table = angle_table(
        jnp.arange(extent_x, dtype=jnp.int32),
        frequency(jnp.arange(MX, dtype=jnp.int32), extent_x, MX),
        extent_x,
    )
    cell_lines = rotate_sum(
        cos_table,
        sin_table,
        lax.all_to_all(y_cells, "gx", split_axis=1, concat_axis=0, tiled=True),
        "xk,kym->xym",
        -1.0,
    )
    planes = lax.all_to_all(cell_lines, "gx", split_axis=0, concat_axis=1, tiled=True)
    z_weights = jnp.where(z_modes_index == 0, 1.0, 2.0).astype(jnp.float32) / (
        extent_x * extent_y * NZ
    )
    planes_split = planes.reshape(cells_x, cells_y, 2, MZ, CH)
    spectral_part = jnp.einsum(
        "xykc,kz->xyzc", planes_split[:, :, 0], z_cos * z_weights[:, None], precision=HIGHEST
    ) - jnp.einsum(
        "xykc,kz->xyzc", planes_split[:, :, 1], z_sin * z_weights[:, None], precision=HIGHEST
    )
    with_rim = with_halo(field, (("gx", 0), ("gy", 1)), 1)
    first_hidden = jax.nn.gelu(convolve(with_rim, conv_first), approximate=False).reshape(
        cells_x, cells_y, merged_width
    )
    hidden_block = with_halo(first_hidden, (("gx", 0), ("gy", 1)), 1)
    second_branch = convolve(hidden_block, conv_second)
    result = jax.nn.gelu(spectral_part + second_branch + bias, approximate=False)
    return result.reshape(cells_x, cells_y, merged_width)


LANES = 256
STEP = LANES // CH
BLOCKS = NZ // STEP
DEPTH = 4 * LANES


def split_bf16(value):
    high = value.astype(jnp.bfloat16)
    low = (value - high.astype(jnp.float32)).astype(jnp.bfloat16)
    return high, low


def erf(value):
    value = jnp.clip(value, -3.832506856900711, 3.832506856900711)
    square = value * value
    top = jnp.float32(0.00022905065861350646)
    for term in (0.0034082910107109506, 0.050955695062380861, 0.18520832239976145, 1.128379143519084):
        top = top * square + term
    bottom = jnp.float32(-1.1791602954361697e-7)
    for term in (0.000023547966471313185, 0.0010179625278914885, 0.014070470171167667, 0.11098505178285362, 0.49746925110067538, 1.0):
        bottom = bottom * square + term
    return value * top / bottom


def gelu(value):
    return value * (1.0 + erf(value * (0.5**0.5))) * 0.5


def conv_kernel(
    body_ref, below_ref, above_ref, tiled_ref, out_ref, b_high, b_low, a_high, a_low, hidden
):
    cells_x, cells_y, _ = body_ref.shape
    place = lax.axis_index("gx")
    last = lax.axis_size("gx") - 1
    lane_block = lax.broadcasted_iota(jnp.int32, (CH, LANES), 1) // CH

    def build_weights(which):
        def per_shift(dx, carry):
            zero = jnp.zeros((CH, LANES), jnp.float32)

            def put(row, value):
                high, low = split_bf16(value)
                b_high[dx, row : row + CH, :] = high
                b_low[dx, row : row + CH, :] = low

            for dy in range(3):
                taps = [tiled_ref[which, dx * 9 + dy * 3 + e] for e in range(3)]
                for i in range(STEP):
                    row = zero
                    for e in range(3):
                        row = jnp.where(lane_block == i + 1 - e, taps[e], row)
                    put(dy * LANES + i * CH, row)
                following = jnp.where(lane_block == STEP - 1, taps[2], 0.0)
                previous = jnp.where(lane_block == 0, taps[0], 0.0)
                offsets = ((0, 96), (64, 32), (128, 224))[dy]
                put(3 * LANES + offsets[0], following)
                put(3 * LANES + offsets[1], previous)
            put(3 * LANES + 160, zero)
            put(3 * LANES + 192, zero)
            return carry

        lax.fori_loop(0, 3, per_shift, 0)

    row_y = lax.broadcasted_iota(jnp.int32, (cells_y, 128), 0)
    lane = lax.broadcasted_iota(jnp.int32, (cells_y, 128), 1)
    row_wide = lax.broadcasted_iota(jnp.int32, (cells_y, LANES), 0)

    def shifted(value, dy, rows):
        if dy == 1:
            return value
        if dy == 0:
            return jnp.where(rows == 0, 0.0, pltpu.roll(value, 1, 0))
        return jnp.where(rows == cells_y - 1, 0.0, pltpu.roll(value, cells_y - 1, 0))

    def build_plane(slot, fetch):
        for b in range(BLOCKS):
            rows = slice(b * cells_y, (b + 1) * cells_y)

            def put(column, value):
                high, low = split_bf16(value)
                width = value.shape[1]
                a_high[slot, rows, column : column + width] = high
                a_low[slot, rows, column : column + width] = low

            main = fetch(b * LANES, LANES)
            edge = jnp.zeros((cells_y, 128), jnp.float32)
            if b > 0:
                edge = jnp.where(lane >= 96, fetch(b * LANES - 128, 128), edge)
            if b < BLOCKS - 1:
                edge = jnp.where(lane < CH, fetch((b + 1) * LANES, 128), edge)
            for dy in range(3):
                put(dy * LANES, shifted(main, dy, row_wide))
            put(3 * LANES, shifted(edge, 0, row_y) + pltpu.roll(edge, 64, 1))
            put(3 * LANES + 128, shifted(edge, 2, row_y))

    def multiply(plane):
        total = jnp.zeros((BLOCKS * cells_y, LANES), jnp.float32)
        for dx in range(3):
            left_high = a_high[plane + dx]
            left_low = a_low[plane + dx]
            right_high = b_high[dx]
            total += jnp.dot(left_high, right_high, preferred_element_type=jnp.float32)
            total += jnp.dot(left_high, b_low[dx], preferred_element_type=jnp.float32)
            total += jnp.dot(left_low, right_high, preferred_element_type=jnp.float32)
        return total

    build_weights(0)

    def from_ref(ref, x, keep):
        def fetch(column, width):
            value = ref[x, :, column : column + width]
            return value if keep is None else jnp.where(keep, value, 0.0)

        return fetch

    def outer(x, carry):
        build_plane(x, from_ref(below_ref, x, place > 0))
        build_plane(cells_x + 2 + x, from_ref(above_ref, x, place < last))
        return carry

    def inner(x, carry):
        build_plane(x + 2, from_ref(body_ref, x, None))
        return carry

    lax.fori_loop(0, 2, outer, 0)
    lax.fori_loop(0, cells_x, inner, 0)

    def first(plane, carry):
        inside = jnp.logical_and(
            jnp.logical_or(plane > 0, place > 0),
            jnp.logical_or(plane < cells_x + 1, place < last),
        )
        hidden[plane] = jnp.where(inside, gelu(multiply(plane)), 0.0)
        return carry

    lax.fori_loop(0, cells_x + 2, first, 0)
    build_weights(1)

    def rebuild(plane, carry):
        def fetch(column, width):
            b = column // LANES
            start = column - b * LANES
            return hidden[plane, b * cells_y : (b + 1) * cells_y, start : start + width]

        build_plane(plane, fetch)
        return carry

    lax.fori_loop(0, cells_x + 2, rebuild, 0)

    def second(plane, carry):
        total = multiply(plane)
        for b in range(BLOCKS):
            out_ref[plane, :, b * LANES : (b + 1) * LANES] = total[b * cells_y : (b + 1) * cells_y]
        return carry

    lax.fori_loop(0, cells_x, second, 0)


def two_convolutions(field, conv_first, conv_second):
    cells_x, cells_y, merged_width = field.shape
    count = lax.axis_size("gx")
    pairs = [(i, i + 1) for i in range(count - 1)]
    below = lax.ppermute(field[cells_x - 2 :], "gx", pairs)
    above = lax.ppermute(field[:2], "gx", [(j, i) for i, j in pairs])
    tiled = jnp.tile(jnp.stack([conv_first, conv_second]).reshape(2, 27, CH, CH), (1, 1, 1, STEP))
    rows = BLOCKS * cells_y
    vmem = pl.BlockSpec(memory_space=pltpu.VMEM)
    flops = 2 * 3 * 3 * (2 * cells_x + 2) * rows * DEPTH * LANES
    return pl.pallas_call(
        conv_kernel,
        out_shape=jax.ShapeDtypeStruct(field.shape, jnp.float32),
        in_specs=[vmem] * 4,
        out_specs=vmem,
        scratch_shapes=[
            pltpu.VMEM((3, DEPTH, LANES), jnp.bfloat16),
            pltpu.VMEM((3, DEPTH, LANES), jnp.bfloat16),
            pltpu.VMEM((cells_x + 4, rows, DEPTH), jnp.bfloat16),
            pltpu.VMEM((cells_x + 4, rows, DEPTH), jnp.bfloat16),
            pltpu.VMEM((cells_x + 2, rows, LANES), jnp.float32),
        ],
        cost_estimate=pl.CostEstimate(flops=flops, bytes_accessed=8 * field.size, transcendentals=0),
        compiler_params=pltpu.CompilerParams(vmem_limit_bytes=28 * 2**20),
    )(field, below, above, tiled)


def mix_kernel(modes_ref, weight_ref, out_ref):
    rows, owned_x, depth = weight_ref.shape[:3]
    mode = 0
    for y in range(rows):
        for x in range(owned_x):
            for k in range(depth):
                real = jnp.broadcast_to(modes_ref[0, 0, :, mode : mode + 1], (CH, CH))
                imag = jnp.broadcast_to(modes_ref[0, 1, :, mode : mode + 1], (CH, CH))
                weight_real = weight_ref[y, x, k, 0]
                weight_imag = weight_ref[y, x, k, 1]
                out_ref[0, 0, mode : mode + 1, :] = jnp.sum(
                    real * weight_real - imag * weight_imag, axis=0, keepdims=True
                )
                out_ref[0, 1, mode : mode + 1, :] = jnp.sum(
                    real * weight_imag + imag * weight_real, axis=0, keepdims=True
                )
                mode += 1


def mix_modes(complex_parts, spectral):
    rows, owned_x = spectral.shape[:2]
    per = 2
    count = per * owned_x * MZ
    steps = rows // per
    modes = complex_parts.reshape(steps, per, owned_x, 2, MZ, CH).transpose(0, 3, 5, 1, 2, 4)
    out = pl.pallas_call(
        mix_kernel,
        grid=(steps,),
        out_shape=jax.ShapeDtypeStruct((steps, 2, count, CH), jnp.float32),
        in_specs=[
            pl.BlockSpec((1, 2, CH, count), lambda i: (i, 0, 0, 0)),
            pl.BlockSpec((per, owned_x, MZ, 2, CH, CH), lambda i: (i, 0, 0, 0, 0, 0)),
        ],
        out_specs=pl.BlockSpec((1, 2, count, CH), lambda i: (i, 0, 0, 0)),
        cost_estimate=pl.CostEstimate(flops=8 * spectral.size, bytes_accessed=16 * spectral.size, transcendentals=0),
    )(modes.reshape(steps, 2, CH, count), spectral)
    return out.reshape(steps, 2, per, owned_x, MZ, CH).transpose(0, 2, 3, 1, 4, 5)


def complex_table(cos_table, sin_table, sign):
    top = jnp.stack([cos_table, sign * sin_table], axis=1)
    bottom = jnp.stack([-sign * sin_table, cos_table], axis=1)
    return jnp.stack([top, bottom], axis=0)


def line_body(field, spectral, conv_first, conv_second, bias):
    cells_x, cells_y, merged_width = field.shape
    devices_x = lax.axis_size("gx")
    extent_x = cells_x * devices_x
    extent_y = cells_y
    owned_x = MX // devices_x
    mode_width = MZ * CH
    second_branch = two_convolutions(field, conv_first, conv_second)
    z_index = jnp.arange(MZ, dtype=jnp.int32)
    z_cos, z_sin = angle_table(z_index, jnp.arange(NZ, dtype=jnp.int32), NZ)
    volume = field.reshape(cells_x, cells_y, NZ, CH)
    forward_z = jnp.stack([z_cos, -z_sin])
    z_spectrum = jnp.einsum("xyzc,rkz->xyrkc", volume, forward_z, precision=HIGH)
    z_spectrum = z_spectrum.reshape(cells_x, cells_y, 2, mode_width)
    kept_x = frequency(jnp.arange(MX, dtype=jnp.int32), extent_x, MX)
    kept_y = frequency(jnp.arange(MY, dtype=jnp.int32), extent_y, MY)
    x_table = complex_table(*angle_table(kept_x, jnp.arange(extent_x, dtype=jnp.int32), extent_x), 1.0)
    y_table = complex_table(*angle_table(kept_y, jnp.arange(extent_y, dtype=jnp.int32), extent_y), 1.0)
    lines = lax.all_to_all(z_spectrum, "gx", split_axis=1, concat_axis=0, tiled=True)
    kept = jnp.einsum("akbx,xybm->kyam", x_table, lines, precision=HIGH)
    x_modes = lax.all_to_all(kept, "gx", split_axis=0, concat_axis=1, tiled=True)
    all_modes = jnp.einsum("akby,xybm->kxam", y_table, x_modes, precision=HIGH)
    mixed = mix_modes(all_modes, spectral).reshape(MY, owned_x, 2, mode_width)
    y_cells = jnp.einsum("bkay,kxbm->xyam", y_table, mixed, precision=HIGH)
    lines = lax.all_to_all(y_cells, "gx", split_axis=1, concat_axis=0, tiled=True)
    lines = jnp.einsum("bkax,kybm->xyam", x_table, lines, precision=HIGH)
    planes = lax.all_to_all(lines, "gx", split_axis=0, concat_axis=1, tiled=True)
    weights = jnp.where(z_index == 0, 1.0, 2.0).astype(jnp.float32) / (extent_x * extent_y * NZ)
    back_z = jnp.stack([z_cos * weights[:, None], -z_sin * weights[:, None]])
    spectral_part = jnp.einsum(
        "xyrkc,rkz->xyzc", planes.reshape(cells_x, cells_y, 2, MZ, CH), back_z, precision=HIGH
    )
    total = spectral_part.reshape(field.shape) + second_branch + jnp.tile(bias, NZ)
    return jax.nn.gelu(total, approximate=False)


def solution(mesh):
    in_specs = (
        P(("groups", "gx"), "gy", None),
        P("gy", "gx", None, None, None, None),
        P(),
        P(),
        P(),
    )
    out_specs = P(("groups", "gx"), "gy", None)
    chosen = line_body if mesh.shape["gy"] == 1 else body
    return jax.shard_map(chosen, mesh=mesh, in_specs=in_specs, out_specs=out_specs, check_vma=False)
```

```python
import functools
import math

import jax
import jax.numpy as jnp
import numpy as np
from jax import lax
from jax.experimental import pallas as pl
from jax.experimental.pallas import tpu as pltpu
from jax.sharding import PartitionSpec as P

CH = 32
NZ = 64
MX = 32
MY = 32
MZ = 16


HIGHEST = lax.Precision.HIGHEST
HIGH = lax.Precision.HIGH


def with_halo(cells, sides, width):
    for axis, dim in sides:
        count = lax.axis_size(axis)
        ends = count - 1
        head = lax.slice_in_dim(cells, 0, width, axis=dim)
        tail = lax.slice_in_dim(cells, cells.shape[dim] - width, cells.shape[dim], axis=dim)
        cells = jnp.concatenate(
            [
                lax.ppermute(tail, axis, [(i, (i + 1) % count) for i in range(ends)]),
                cells,
                lax.ppermute(head, axis, [((i + 1) % count, i) for i in range(ends)]),
            ],
            axis=dim,
        )
    return cells


def frequency(position, length, retained):
    return jnp.where(position < retained // 2, position, length - retained + position)


def angle_table(first_list, second_list, length):
    product = first_list[:, None] * second_list[None, :] % length
    angles = product.astype(jnp.float32) * (2.0 * math.pi / length)
    return (jnp.cos(angles), jnp.sin(angles))


def rotate_sum(cos_table, sin_table, values, pattern, direction_sign):
    real_part = values[:, :, 0]
    imag_part = values[:, :, 1]
    out_real = jnp.einsum(
        pattern, cos_table, real_part, precision=HIGHEST
    ) + direction_sign * jnp.einsum(pattern, sin_table, imag_part, precision=HIGHEST)
    out_imag = jnp.einsum(
        pattern, cos_table, imag_part, precision=HIGHEST
    ) - direction_sign * jnp.einsum(pattern, sin_table, real_part, precision=HIGHEST)
    return jnp.stack([out_real, out_imag], axis=2)


def convolve(padded, weight):
    extent_x = padded.shape[0] - 2
    extent_y = padded.shape[1] - 2
    volume = padded.reshape(padded.shape[0], padded.shape[1], NZ, CH)
    volume = jnp.pad(volume, ((0, 0), (0, 0), (1, 1), (0, 0)))
    kernel = weight.reshape(3, 3, 3 * CH, CH)

    def plane(start):
        slab = lax.dynamic_slice_in_dim(volume, start, 3, 0)
        accumulated = jnp.zeros((extent_y, NZ, CH), jnp.float32)
        for shift_x in range(3):
            for shift_y in range(3):
                windowed = slab[shift_x, shift_y : shift_y + extent_y]
                stacked = jnp.concatenate(
                    [windowed[:, shift_z : shift_z + NZ] for shift_z in range(3)], axis=2
                )
                accumulated = accumulated + jnp.einsum(
                    "yzi,io->yzo", stacked, kernel[shift_x, shift_y], precision=HIGHEST
                )
        return accumulated

    return lax.map(plane, jnp.arange(extent_x, dtype=jnp.int32))


def mode_mix(inputs, matrix):
    return jnp.einsum("bazi,bazio->bazo", inputs, matrix, precision=HIGHEST)


def body(field, spectral, conv_first, conv_second, bias):
    cells_x, cells_y, merged_width = field.shape
    devices_x = lax.axis_size("gx")
    devices_y = lax.axis_size("gy")
    extent_x = cells_x * devices_x
    extent_y = cells_y * devices_y
    owned_x = MX // devices_x
    owned_y = MY // devices_y
    y_places = lax.axis_index("gy") * cells_y + jnp.arange(cells_y, dtype=jnp.int32)
    mode_width = MZ * CH
    volume = field.reshape(cells_x, cells_y, NZ, CH)
    z_modes_index = jnp.arange(MZ, dtype=jnp.int32)
    z_cos, z_sin = angle_table(z_modes_index, jnp.arange(NZ, dtype=jnp.int32), NZ)
    z_real = jnp.einsum("xyzc,kz->xykc", volume, z_cos, precision=HIGHEST)
    z_imag = -jnp.einsum("xyzc,kz->xykc", volume, z_sin, precision=HIGHEST)
    z_spectrum = jnp.stack([z_real, z_imag], axis=2).reshape(cells_x, cells_y, 2, mode_width)
    cos_table, sin_table = angle_table(
        frequency(jnp.arange(MX, dtype=jnp.int32), extent_x, MX),
        jnp.arange(extent_x, dtype=jnp.int32),
        extent_x,
    )
    kept_modes = rotate_sum(
        cos_table,
        sin_table,
        lax.all_to_all(z_spectrum, "gx", split_axis=1, concat_axis=0, tiled=True),
        "kx,xym->kym",
        1.0,
    )
    x_modes = lax.all_to_all(kept_modes, "gx", split_axis=0, concat_axis=1, tiled=True)
    row_index = jnp.arange(owned_y * lax.axis_size("gy"), dtype=jnp.int32)
    cos_table, sin_table = angle_table(frequency(row_index, extent_y, MY), y_places, extent_y)
    all_modes = lax.psum_scatter(
        rotate_sum(cos_table, sin_table, x_modes, "ky,xym->kxm", 1.0),
        "gy",
        scatter_dimension=0,
        tiled=True,
    )
    complex_parts = all_modes.reshape(owned_y, owned_x, 2, MZ, CH)
    real_inputs = complex_parts[:, :, 0]
    imag_inputs = complex_parts[:, :, 1]
    weight_real = spectral[:, :, :, 0]
    weight_imag = spectral[:, :, :, 1]
    mixed_real = mode_mix(real_inputs, weight_real) - mode_mix(imag_inputs, weight_imag)
    mixed_imag = mode_mix(real_inputs, weight_imag) + mode_mix(imag_inputs, weight_real)
    mixed = jnp.stack([mixed_real, mixed_imag], axis=2).reshape(owned_y, owned_x, 2, mode_width)
    portion = lax.all_gather(mixed, "gy", axis=0, tiled=True)
    row_index = jnp.arange(portion.shape[0], dtype=jnp.int32)
    cos_table, sin_table = angle_table(y_places, frequency(row_index, extent_y, MY), extent_y)
    y_cells = rotate_sum(cos_table, sin_table, portion, "yk,kxm->xym", -1.0)
    cos_table, sin_table = angle_table(
        jnp.arange(extent_x, dtype=jnp.int32),
        frequency(jnp.arange(MX, dtype=jnp.int32), extent_x, MX),
        extent_x,
    )
    cell_lines = rotate_sum(
        cos_table,
        sin_table,
        lax.all_to_all(y_cells, "gx", split_axis=1, concat_axis=0, tiled=True),
        "xk,kym->xym",
        -1.0,
    )
    planes = lax.all_to_all(cell_lines, "gx", split_axis=0, concat_axis=1, tiled=True)
    z_weights = jnp.where(z_modes_index == 0, 1.0, 2.0).astype(jnp.float32) / (
        extent_x * extent_y * NZ
    )
    planes_split = planes.reshape(cells_x, cells_y, 2, MZ, CH)
    spectral_part = jnp.einsum(
        "xykc,kz->xyzc", planes_split[:, :, 0], z_cos * z_weights[:, None], precision=HIGHEST
    ) - jnp.einsum(
        "xykc,kz->xyzc", planes_split[:, :, 1], z_sin * z_weights[:, None], precision=HIGHEST
    )
    with_rim = with_halo(field, (("gx", 0), ("gy", 1)), 1)
    first_hidden = jax.nn.gelu(convolve(with_rim, conv_first), approximate=False).reshape(
        cells_x, cells_y, merged_width
    )
    hidden_block = with_halo(first_hidden, (("gx", 0), ("gy", 1)), 1)
    second_branch = convolve(hidden_block, conv_second)
    result = jax.nn.gelu(spectral_part + second_branch + bias, approximate=False)
    return result.reshape(cells_x, cells_y, merged_width)


LANES = 256
STEP = LANES // CH
BLOCKS = NZ // STEP
DEPTH = 4 * LANES


def split_bf16(value):
    high = value.astype(jnp.bfloat16)
    low = (value - high.astype(jnp.float32)).astype(jnp.bfloat16)
    return high, low


def erf(value):
    value = jnp.clip(value, -3.832506856900711, 3.832506856900711)
    square = value * value
    top = jnp.float32(0.00022905065861350646)
    for term in (0.0034082910107109506, 0.050955695062380861, 0.18520832239976145, 1.128379143519084):
        top = top * square + term
    bottom = jnp.float32(-1.1791602954361697e-7)
    for term in (0.000023547966471313185, 0.0010179625278914885, 0.014070470171167667, 0.11098505178285362, 0.49746925110067538, 1.0):
        bottom = bottom * square + term
    return value * top / bottom


def gelu(value):
    return value * (1.0 + erf(value * (0.5**0.5))) * 0.5


MESH = pl.DeviceIdType.MESH


def block_kernel(
    count, body_ref, spectral_ref, first_ref, second_ref, bias_ref, z_ref, scale_ref,
    x_in_ref, y_in_ref, y_out_ref, x_out_ref, out_ref,
    b_high, b_low, a_high, a_low, hidden, z_high, z_low, weights, modes, mixed, spectrum,
    below, above, sends, lands, send_sems, land_sems, halo_send, halo_land, weight_sem,
):
    cells_x, cells_y, merged_width = body_ref.shape
    owned_x = spectral_ref.shape[1]
    mode_width = MZ * CH
    block = sends.shape[1] // count
    place = lax.axis_index("gx")
    last = count - 1

    barrier = pltpu.get_barrier_semaphore()
    for offset in range(1, count):
        pl.semaphore_signal(
            barrier, inc=1, device_id={"gx": lax.rem(place + offset, count)}, device_id_type=MESH
        )
    weight_copy = pltpu.make_async_copy(spectral_ref, weights, weight_sem)
    weight_copy.start()

    def at(index):
        return pl.ds(pl.multiple_of(index * block, 8), block)

    def exchange(stage):
        copies = []
        for offset in [o for k in range(count // 2, 0, -1) for o in sorted({k, count - k})]:
            peer = lax.rem(place + offset, count)
            copy = pltpu.make_async_remote_copy(
                src_ref=sends.at[stage, at(peer)],
                dst_ref=lands.at[stage, at(place)],
                send_sem=send_sems.at[stage, offset],
                recv_sem=land_sems.at[stage, offset],
                device_id={"gx": peer},
                device_id_type=MESH,
            )
            copy.start()
            copies.append(copy)
        lands[stage, at(place), :] = sends[stage, at(place), :]
        return copies

    def finish(copies):
        for copy in copies:
            copy.wait()

    def build_z(z, carry):
        row = z_ref[pl.ds(z, 1), :]
        high = row.astype(jnp.bfloat16).astype(jnp.float32)
        low = row - high
        lane = lax.broadcasted_iota(jnp.int32, (CH, 2 * mode_width), 1)
        keep = lane % CH == lax.broadcasted_iota(jnp.int32, (CH, 2 * mode_width), 0)
        rows = pl.ds(pl.multiple_of(z * CH, CH), CH)
        z_high[rows, :] = jnp.where(keep, high, 0.0).astype(jnp.bfloat16)
        z_low[rows, :] = jnp.where(keep, low, 0.0).astype(jnp.bfloat16)
        return carry

    lax.fori_loop(0, NZ, build_z, 0)
    data_high, data_low = split_bf16(body_ref[...].reshape(cells_x * cells_y, merged_width))
    for ri in range(2):
        columns = slice(ri * mode_width, (ri + 1) * mode_width)
        part = jnp.dot(data_high, z_high[:, columns], preferred_element_type=jnp.float32)
        part += jnp.dot(data_high, z_low[:, columns], preferred_element_type=jnp.float32)
        part += jnp.dot(data_low, z_high[:, columns], preferred_element_type=jnp.float32)
        for x in range(cells_x):
            rows = pl.ds(x * 2 + ri, cells_y, stride=2 * cells_x)
            for q in range(mode_width // 128):
                lanes = slice(q * 128, (q + 1) * 128)
                spectrum[q, rows, :] = part[x * cells_y : (x + 1) * cells_y, lanes]
    for q in range(mode_width // 128):
        sends[0, :, q * 128 : (q + 1) * 128] = spectrum[q]

    pl.semaphore_wait(barrier, count - 1)
    copies = exchange(0)

    up = pltpu.make_async_remote_copy(
        src_ref=body_ref.at[pl.ds(cells_x - 2, 2)], dst_ref=below, send_sem=halo_send.at[0],
        recv_sem=halo_land.at[0], device_id={"gx": lax.rem(place + 1, count)}, device_id_type=MESH,
    )
    down = pltpu.make_async_remote_copy(
        src_ref=body_ref.at[pl.ds(0, 2)], dst_ref=above, send_sem=halo_send.at[1],
        recv_sem=halo_land.at[1], device_id={"gx": lax.rem(place + last, count)}, device_id_type=MESH,
    )

    @pl.when(place < last)
    def _():
        up.start()

    @pl.when(place > 0)
    def _():
        down.start()

    lane_block = lax.broadcasted_iota(jnp.int32, (CH, LANES), 1) // CH

    def build_weights(tap_ref):
        def per_shift(dx, carry):
            zero = jnp.zeros((CH, LANES), jnp.float32)

            def put(row, value):
                high, low = split_bf16(value)
                b_high[dx, row : row + CH, :] = high
                b_low[dx, row : row + CH, :] = low

            for dy in range(3):
                taps = [
                    jnp.concatenate([tap_ref[dx * 9 + dy * 3 + e]] * STEP, axis=1) for e in range(3)
                ]
                for i in range(STEP):
                    row = zero
                    for e in range(3):
                        row = jnp.where(lane_block == i + 1 - e, taps[e], row)
                    put(dy * LANES + i * CH, row)
                following = jnp.where(lane_block == STEP - 1, taps[2], 0.0)
                previous = jnp.where(lane_block == 0, taps[0], 0.0)
                offsets = ((0, 96), (64, 32), (128, 224))[dy]
                put(3 * LANES + offsets[0], following)
                put(3 * LANES + offsets[1], previous)
            put(3 * LANES + 160, zero)
            put(3 * LANES + 192, zero)
            return carry

        lax.fori_loop(0, 3, per_shift, 0)

    row_y = lax.broadcasted_iota(jnp.int32, (cells_y, 128), 0)
    lane = lax.broadcasted_iota(jnp.int32, (cells_y, 128), 1)
    row_wide = lax.broadcasted_iota(jnp.int32, (cells_y, LANES), 0)

    def shifted(value, dy, rows):
        if dy == 1:
            return value
        if dy == 0:
            return jnp.where(rows == 0, 0.0, pltpu.roll(value, 1, 0))
        return jnp.where(rows == cells_y - 1, 0.0, pltpu.roll(value, cells_y - 1, 0))

    def build_plane(slot, fetch):
        for b in range(BLOCKS):
            rows = slice(b * cells_y, (b + 1) * cells_y)

            def put(column, value):
                high, low = split_bf16(value)
                width = value.shape[1]
                a_high[slot, rows, column : column + width] = high
                a_low[slot, rows, column : column + width] = low

            main = fetch(b * LANES, LANES)
            edge = jnp.zeros((cells_y, 128), jnp.float32)
            if b > 0:
                edge = jnp.where(lane >= 96, fetch(b * LANES - 128, 128), edge)
            if b < BLOCKS - 1:
                edge = jnp.where(lane < CH, fetch((b + 1) * LANES, 128), edge)
            for dy in range(3):
                put(dy * LANES, shifted(main, dy, row_wide))
            put(3 * LANES, shifted(edge, 0, row_y) + pltpu.roll(edge, 64, 1))
            put(3 * LANES + 128, shifted(edge, 2, row_y))

    def multiply(plane):
        total = jnp.zeros((BLOCKS * cells_y, LANES), jnp.float32)
        for dx in range(3):
            left_high = a_high[plane + dx]
            left_low = a_low[plane + dx]
            right_high = b_high[dx]
            total += jnp.dot(left_high, right_high, preferred_element_type=jnp.float32)
            total += jnp.dot(left_high, b_low[dx], preferred_element_type=jnp.float32)
            total += jnp.dot(left_low, right_high, preferred_element_type=jnp.float32)
        return total

    def from_ref(ref, x):
        return lambda column, width: ref[x, :, column : column + width]

    def inner(x, carry):
        build_plane(x + 2, from_ref(body_ref, x))
        return carry

    def lower(x, carry):
        build_plane(x, from_ref(below, x))
        return carry

    def upper(x, carry):
        build_plane(cells_x + 2 + x, from_ref(above, x))
        return carry

    build_weights(first_ref)
    lax.fori_loop(0, cells_x, inner, 0)

    finish(copies)
    sends[1] = jnp.dot(x_in_ref[...], lands[0], precision=HIGHEST, preferred_element_type=jnp.float32)
    copies = exchange(1)

    @pl.when(place < last)
    def _():
        up.wait_send()
        down.wait_recv()

    @pl.when(place == last)
    def _():
        above[...] = jnp.zeros_like(above)

    @pl.when(place > 0)
    def _():
        down.wait_send()
        up.wait_recv()

    @pl.when(place == 0)
    def _():
        below[...] = jnp.zeros_like(below)

    lax.fori_loop(0, 2, lower, 0)
    lax.fori_loop(0, 2, upper, 0)

    def first(plane, carry):
        inside = jnp.logical_and(
            jnp.logical_or(plane > 0, place > 0),
            jnp.logical_or(plane < cells_x + 1, place < last),
        )
        hidden[plane] = jnp.where(inside, gelu(multiply(plane)), 0.0)
        return carry

    lax.fori_loop(0, cells_x + 2, first, 0)

    finish(copies)
    modes[...] = lax.dot_general(
        lands[1], y_in_ref[...], (((0,), (1,)), ((), ())),
        precision=HIGHEST, preferred_element_type=jnp.float32,
    )
    weight_copy.wait()
    group = 4

    def mix_rows(step, carry):
        q = step % (MZ // 4)
        g = step // (MZ // 4)
        lines = pl.ds(pl.multiple_of(q * 128, 128), 128)
        width = group * owned_x * 2
        cols = pltpu.roll(modes[lines, :], lax.rem(modes.shape[1] - g * width, modes.shape[1]), 1)
        for y in range(group):
            for x in range(owned_x):
                spot = (y * owned_x + x) * 2
                reals, imags = [], []
                for k in range(4):
                    real = jnp.broadcast_to(cols[k * CH : (k + 1) * CH, spot : spot + 1], (CH, CH))
                    imag = jnp.broadcast_to(cols[k * CH : (k + 1) * CH, spot + 1 : spot + 2], (CH, CH))
                    weight_real = weights[g * group + y, x, q * 4 + k, 0]
                    weight_imag = weights[g * group + y, x, q * 4 + k, 1]
                    out_real = real * weight_real - imag * weight_imag
                    out_imag = real * weight_imag + imag * weight_real
                    reals.append(out_real.reshape(CH // 8, 8, CH).sum(0))
                    imags.append(out_imag.reshape(CH // 8, 8, CH).sum(0))
                for ri, parts in enumerate((reals, imags)):
                    mixed[q, pl.ds(g * width + spot + ri, 1), :] = jnp.sum(
                        jnp.concatenate(parts, axis=1), axis=0, keepdims=True
                    )
        return carry

    lax.fori_loop(0, (MZ // 4) * (MY // group), mix_rows, 0)
    for q in range(MZ // 4):
        sends[2, :, q * 128 : (q + 1) * 128] = jnp.dot(
            y_out_ref[...], mixed[q], precision=HIGHEST, preferred_element_type=jnp.float32
        )
    copies = exchange(2)

    build_weights(second_ref)

    def rebuild(plane, carry):
        def fetch(column, width):
            b = column // LANES
            start = column - b * LANES
            return hidden[plane, b * cells_y : (b + 1) * cells_y, start : start + width]

        build_plane(plane, fetch)
        return carry

    lax.fori_loop(0, cells_x + 2, rebuild, 0)

    finish(copies)
    sends[3] = jnp.dot(x_out_ref[...], lands[2], precision=HIGHEST, preferred_element_type=jnp.float32)
    copies = exchange(3)

    def second(plane, carry):
        total = multiply(plane)
        for b in range(BLOCKS):
            out_ref[plane, :, b * LANES : (b + 1) * LANES] = (
                total[b * cells_y : (b + 1) * cells_y] + bias_ref[...]
            )
        return carry

    lax.fori_loop(0, cells_x, second, 0)

    finish(copies)
    for q in range(mode_width // 128):
        spectrum[q] = lands[3, :, q * 128 : (q + 1) * 128]
    lines = []
    for x in range(cells_x):
        lines.append(
            jnp.concatenate(
                [
                    spectrum[q, pl.ds(x * 2 + ri, cells_y, stride=2 * cells_x), :]
                    for ri in range(2)
                    for q in range(mode_width // 128)
                ],
                axis=1,
            )
        )
    line_high, line_low = split_bf16(jnp.concatenate(lines, axis=0) * scale_ref[...])
    across = (((1,), (1,)), ((), ()))
    for b in range(BLOCKS):
        rows = slice(b * LANES, (b + 1) * LANES)
        part = lax.dot_general(line_high, z_high[rows, :], across, preferred_element_type=jnp.float32)
        part += lax.dot_general(line_high, z_low[rows, :], across, preferred_element_type=jnp.float32)
        part += lax.dot_general(line_low, z_high[rows, :], across, preferred_element_type=jnp.float32)
        for x in range(cells_x):
            out_ref[x, :, rows] = gelu(out_ref[x, :, rows] + part[x * cells_y : (x + 1) * cells_y])


def kept_list(length, retained):
    spots = np.arange(retained)
    return np.where(spots < retained // 2, spots, length - retained + spots)


def rotation(angle_index, length, inverse):
    angle = angle_index % length * (2.0 * math.pi / length)
    cos, sin = np.cos(angle), np.sin(angle)
    sign = -1.0 if inverse else 1.0
    return np.stack([np.stack([cos, sign * sin], -1), np.stack([-sign * sin, cos], -1)], -2)


def tables(cells_x, cells_y, count):
    extent_x, owned_x, rows_y = cells_x * count, MX // count, cells_y // count
    x_turn = rotation(kept_list(extent_x, MX)[:, None] * np.arange(extent_x)[None], extent_x, False)
    y_turn = rotation(kept_list(cells_y, MY)[:, None] * np.arange(cells_y)[None], cells_y, False)
    x_turn = x_turn.reshape(count, owned_x, count, cells_x, 2, 2)
    y_turn = y_turn.reshape(MY, count, rows_y, 2, 2)
    same_y, same_x = np.eye(rows_y), np.eye(owned_x)
    x_in = np.einsum("ekdxab,yw->ekyadwxb", x_turn, same_y).reshape(count * owned_x * rows_y * 2, -1)
    y_in = np.einsum("ldyab,kj->lkadjyb", y_turn, same_x).reshape(MY * owned_x * 2, -1)
    y_out = np.einsum("leyba,kj->eykaljb", y_turn, same_x).reshape(count * rows_y * owned_x * 2, -1)
    x_out = np.einsum("dkexba,yw->eyxadwkb", x_turn, same_y).reshape(count * rows_y * cells_x * 2, -1)
    angle = np.arange(NZ)[:, None] * np.arange(MZ)[None] % NZ * (2.0 * math.pi / NZ)
    z_table = np.repeat(np.stack([np.cos(angle), -np.sin(angle)], 1).reshape(NZ, 2 * MZ), CH, axis=1)
    scale = np.where(np.arange(MZ) == 0, 1.0, 2.0) / (extent_x * cells_y * NZ)
    scale = np.repeat(np.tile(scale, 2), CH)[None]
    return [jnp.asarray(t, jnp.float32) for t in (z_table, scale, x_in, y_in, y_out, x_out)]


def line_body(field, spectral, conv_first, conv_second, bias):
    cells_x, cells_y, merged_width = field.shape
    count = lax.axis_size("gx")
    mode_width = MZ * CH
    total_rows = cells_x * cells_y * 2
    rows = BLOCKS * cells_y
    vmem = pl.BlockSpec(memory_space=pltpu.VMEM)
    quarter = mode_width // 128
    return pl.pallas_call(
        functools.partial(block_kernel, count),
        out_shape=jax.ShapeDtypeStruct(field.shape, jnp.float32),
        in_specs=[vmem, pl.BlockSpec(memory_space=pl.ANY)] + [vmem] * 9,
        out_specs=vmem,
        scratch_shapes=[
            pltpu.VMEM((3, DEPTH, LANES), jnp.bfloat16),
            pltpu.VMEM((3, DEPTH, LANES), jnp.bfloat16),
            pltpu.VMEM((cells_x + 4, rows, DEPTH), jnp.bfloat16),
            pltpu.VMEM((cells_x + 4, rows, DEPTH), jnp.bfloat16),
            pltpu.VMEM((cells_x + 2, rows, LANES), jnp.float32),
            pltpu.VMEM((merged_width, 2 * mode_width), jnp.bfloat16),
            pltpu.VMEM((merged_width, 2 * mode_width), jnp.bfloat16),
            pltpu.VMEM(spectral.shape, jnp.float32),
            pltpu.VMEM((mode_width, total_rows), jnp.float32),
            pltpu.VMEM((quarter, total_rows, 128), jnp.float32),
            pltpu.VMEM((quarter, total_rows, 128), jnp.float32),
            pltpu.VMEM((2, cells_y, merged_width), jnp.float32),
            pltpu.VMEM((2, cells_y, merged_width), jnp.float32),
            pltpu.VMEM((4, total_rows, mode_width), jnp.float32),
            pltpu.VMEM((4, total_rows, mode_width), jnp.float32),
            pltpu.SemaphoreType.DMA((4, count)),
            pltpu.SemaphoreType.DMA((4, count)),
            pltpu.SemaphoreType.DMA((2,)),
            pltpu.SemaphoreType.DMA((2,)),
            pltpu.SemaphoreType.DMA,
        ],
        compiler_params=pltpu.CompilerParams(
            collective_id=0, has_side_effects=True, vmem_limit_bytes=63 * 2**20
        ),
    )(
        field, spectral, conv_first.reshape(27, CH, CH), conv_second.reshape(27, CH, CH),
        jnp.tile(bias, STEP)[None], *tables(cells_x, cells_y, count),
    )


def solution(mesh):
    in_specs = (
        P(("groups", "gx"), "gy", None),
        P("gy", "gx", None, None, None, None),
        P(),
        P(),
        P(),
    )
    out_specs = P(("groups", "gx"), "gy", None)
    count = mesh.shape["gx"]

    def chosen(field, *rest):
        whole = (field.shape[0] * count, field.shape[1] * mesh.shape["gy"])
        fits = whole == (MX, MY) and mesh.shape["gy"] == 1 and MX == MY == 2 * count
        return (line_body if fits else body)(field, *rest)

    return jax.shard_map(chosen, mesh=mesh, in_specs=in_specs, out_specs=out_specs, check_vma=False)
```

```python
import functools
import math

import jax
import jax.numpy as jnp
import numpy as np
from jax import lax
from jax.experimental import pallas as pl
from jax.experimental.pallas import tpu as pltpu
from jax.sharding import PartitionSpec as P

CH = 32
NZ = 64
MX = 32
MY = 32
MZ = 16


HIGHEST = lax.Precision.HIGHEST
HIGH = lax.Precision.HIGH


def with_halo(cells, sides, width):
    for axis, dim in sides:
        count = lax.axis_size(axis)
        ends = count - 1
        head = lax.slice_in_dim(cells, 0, width, axis=dim)
        tail = lax.slice_in_dim(cells, cells.shape[dim] - width, cells.shape[dim], axis=dim)
        cells = jnp.concatenate(
            [
                lax.ppermute(tail, axis, [(i, (i + 1) % count) for i in range(ends)]),
                cells,
                lax.ppermute(head, axis, [((i + 1) % count, i) for i in range(ends)]),
            ],
            axis=dim,
        )
    return cells


def frequency(position, length, retained):
    return jnp.where(position < retained // 2, position, length - retained + position)


def angle_table(first_list, second_list, length):
    product = first_list[:, None] * second_list[None, :] % length
    angles = product.astype(jnp.float32) * (2.0 * math.pi / length)
    return (jnp.cos(angles), jnp.sin(angles))


def rotate_sum(cos_table, sin_table, values, pattern, direction_sign):
    real_part = values[:, :, 0]
    imag_part = values[:, :, 1]
    out_real = jnp.einsum(
        pattern, cos_table, real_part, precision=HIGHEST
    ) + direction_sign * jnp.einsum(pattern, sin_table, imag_part, precision=HIGHEST)
    out_imag = jnp.einsum(
        pattern, cos_table, imag_part, precision=HIGHEST
    ) - direction_sign * jnp.einsum(pattern, sin_table, real_part, precision=HIGHEST)
    return jnp.stack([out_real, out_imag], axis=2)


def convolve(padded, weight):
    extent_x = padded.shape[0] - 2
    extent_y = padded.shape[1] - 2
    volume = padded.reshape(padded.shape[0], padded.shape[1], NZ, CH)
    volume = jnp.pad(volume, ((0, 0), (0, 0), (1, 1), (0, 0)))
    kernel = weight.reshape(3, 3, 3 * CH, CH)

    def plane(start):
        slab = lax.dynamic_slice_in_dim(volume, start, 3, 0)
        accumulated = jnp.zeros((extent_y, NZ, CH), jnp.float32)
        for shift_x in range(3):
            for shift_y in range(3):
                windowed = slab[shift_x, shift_y : shift_y + extent_y]
                stacked = jnp.concatenate(
                    [windowed[:, shift_z : shift_z + NZ] for shift_z in range(3)], axis=2
                )
                accumulated = accumulated + jnp.einsum(
                    "yzi,io->yzo", stacked, kernel[shift_x, shift_y], precision=HIGHEST
                )
        return accumulated

    return lax.map(plane, jnp.arange(extent_x, dtype=jnp.int32))


def mode_mix(inputs, matrix):
    return jnp.einsum("bazi,bazio->bazo", inputs, matrix, precision=HIGHEST)


def body(field, spectral, conv_first, conv_second, bias):
    cells_x, cells_y, merged_width = field.shape
    devices_x = lax.axis_size("gx")
    devices_y = lax.axis_size("gy")
    extent_x = cells_x * devices_x
    extent_y = cells_y * devices_y
    owned_x = MX // devices_x
    owned_y = MY // devices_y
    y_places = lax.axis_index("gy") * cells_y + jnp.arange(cells_y, dtype=jnp.int32)
    mode_width = MZ * CH
    volume = field.reshape(cells_x, cells_y, NZ, CH)
    z_modes_index = jnp.arange(MZ, dtype=jnp.int32)
    z_cos, z_sin = angle_table(z_modes_index, jnp.arange(NZ, dtype=jnp.int32), NZ)
    z_real = jnp.einsum("xyzc,kz->xykc", volume, z_cos, precision=HIGHEST)
    z_imag = -jnp.einsum("xyzc,kz->xykc", volume, z_sin, precision=HIGHEST)
    z_spectrum = jnp.stack([z_real, z_imag], axis=2).reshape(cells_x, cells_y, 2, mode_width)
    cos_table, sin_table = angle_table(
        frequency(jnp.arange(MX, dtype=jnp.int32), extent_x, MX),
        jnp.arange(extent_x, dtype=jnp.int32),
        extent_x,
    )
    kept_modes = rotate_sum(
        cos_table,
        sin_table,
        lax.all_to_all(z_spectrum, "gx", split_axis=1, concat_axis=0, tiled=True),
        "kx,xym->kym",
        1.0,
    )
    x_modes = lax.all_to_all(kept_modes, "gx", split_axis=0, concat_axis=1, tiled=True)
    row_index = jnp.arange(owned_y * lax.axis_size("gy"), dtype=jnp.int32)
    cos_table, sin_table = angle_table(frequency(row_index, extent_y, MY), y_places, extent_y)
    all_modes = lax.psum_scatter(
        rotate_sum(cos_table, sin_table, x_modes, "ky,xym->kxm", 1.0),
        "gy",
        scatter_dimension=0,
        tiled=True,
    )
    complex_parts = all_modes.reshape(owned_y, owned_x, 2, MZ, CH)
    real_inputs = complex_parts[:, :, 0]
    imag_inputs = complex_parts[:, :, 1]
    weight_real = spectral[:, :, :, 0]
    weight_imag = spectral[:, :, :, 1]
    mixed_real = mode_mix(real_inputs, weight_real) - mode_mix(imag_inputs, weight_imag)
    mixed_imag = mode_mix(real_inputs, weight_imag) + mode_mix(imag_inputs, weight_real)
    mixed = jnp.stack([mixed_real, mixed_imag], axis=2).reshape(owned_y, owned_x, 2, mode_width)
    portion = lax.all_gather(mixed, "gy", axis=0, tiled=True)
    row_index = jnp.arange(portion.shape[0], dtype=jnp.int32)
    cos_table, sin_table = angle_table(y_places, frequency(row_index, extent_y, MY), extent_y)
    y_cells = rotate_sum(cos_table, sin_table, portion, "yk,kxm->xym", -1.0)
    cos_table, sin_table = angle_table(
        jnp.arange(extent_x, dtype=jnp.int32),
        frequency(jnp.arange(MX, dtype=jnp.int32), extent_x, MX),
        extent_x,
    )
    cell_lines = rotate_sum(
        cos_table,
        sin_table,
        lax.all_to_all(y_cells, "gx", split_axis=1, concat_axis=0, tiled=True),
        "xk,kym->xym",
        -1.0,
    )
    planes = lax.all_to_all(cell_lines, "gx", split_axis=0, concat_axis=1, tiled=True)
    z_weights = jnp.where(z_modes_index == 0, 1.0, 2.0).astype(jnp.float32) / (
        extent_x * extent_y * NZ
    )
    planes_split = planes.reshape(cells_x, cells_y, 2, MZ, CH)
    spectral_part = jnp.einsum(
        "xykc,kz->xyzc", planes_split[:, :, 0], z_cos * z_weights[:, None], precision=HIGHEST
    ) - jnp.einsum(
        "xykc,kz->xyzc", planes_split[:, :, 1], z_sin * z_weights[:, None], precision=HIGHEST
    )
    with_rim = with_halo(field, (("gx", 0), ("gy", 1)), 1)
    first_hidden = jax.nn.gelu(convolve(with_rim, conv_first), approximate=False).reshape(
        cells_x, cells_y, merged_width
    )
    hidden_block = with_halo(first_hidden, (("gx", 0), ("gy", 1)), 1)
    second_branch = convolve(hidden_block, conv_second)
    result = jax.nn.gelu(spectral_part + second_branch + bias, approximate=False)
    return result.reshape(cells_x, cells_y, merged_width)


LANES = 256
STEP = LANES // CH
BLOCKS = NZ // STEP
DEPTH = 4 * LANES


def split_bf16(value):
    high = value.astype(jnp.bfloat16)
    low = (value - high.astype(jnp.float32)).astype(jnp.bfloat16)
    return high, low


def erf(value):
    value = jnp.clip(value, -3.832506856900711, 3.832506856900711)
    square = value * value
    top = jnp.float32(0.00022905065861350646)
    for term in (0.0034082910107109506, 0.050955695062380861, 0.18520832239976145, 1.128379143519084):
        top = top * square + term
    bottom = jnp.float32(-1.1791602954361697e-7)
    for term in (0.000023547966471313185, 0.0010179625278914885, 0.014070470171167667, 0.11098505178285362, 0.49746925110067538, 1.0):
        bottom = bottom * square + term
    return value * top / bottom


def gelu(value):
    return value * (1.0 + erf(value * (0.5**0.5))) * 0.5


MESH = pl.DeviceIdType.MESH


def block_kernel(
    count, body_ref, spectral_ref, first_ref, second_ref, bias_ref, z_ref, scale_ref,
    x_in_ref, y_in_ref, y_out_ref, x_out_ref, out_ref,
    b_high, b_low, a_high, a_low, hidden, z_high, z_low, slots, packed, spectrum,
    below, above, sends, lands, send_sems, land_sems, halo_send, halo_land, weight_sem,
):
    cells_x, cells_y, merged_width = body_ref.shape
    owned_x = spectral_ref.shape[1]
    mode_width = MZ * CH
    block = sends.shape[1] // count
    place = lax.axis_index("gx")
    last = count - 1

    barrier = pltpu.get_barrier_semaphore()
    for offset in range(1, count):
        pl.semaphore_signal(
            barrier, inc=1, device_id={"gx": lax.rem(place + offset, count)}, device_id_type=MESH
        )
    slot_count, per_slot = slots.shape[:2]
    chunks = MY // per_slot
    pairs = MY * owned_x
    quarter = mode_width // 128

    def weight_copy(chunk):
        slot = lax.rem(chunk, slot_count)
        return pltpu.make_async_copy(
            spectral_ref.at[pl.ds(chunk * per_slot, per_slot)], slots.at[slot], weight_sem.at[slot]
        )

    for chunk in range(slot_count):
        weight_copy(chunk).start()

    def pack(chunk, carry):
        weight_copy(chunk).wait()
        slot = lax.rem(chunk, slot_count)
        for y in range(per_slot):
            for x in range(owned_x):
                pair = (chunk * per_slot + y) * owned_x + x
                for q in range(quarter):
                    for ri in range(2):
                        tile = jnp.concatenate([slots[slot, y, x, q * 4 + k, ri] for k in range(4)], axis=0)
                        packed[q, ri, pl.ds(pair, CH, stride=pairs), :] = tile.T

        @pl.when(chunk + slot_count < chunks)
        def _():
            weight_copy(chunk + slot_count).start()

        return carry

    def at(index):
        return pl.ds(pl.multiple_of(index * block, 8), block)

    def exchange(stage):
        copies = []
        for offset in [o for k in range(count // 2, 0, -1) for o in sorted({k, count - k})]:
            peer = lax.rem(place + offset, count)
            copy = pltpu.make_async_remote_copy(
                src_ref=sends.at[stage, at(peer)],
                dst_ref=lands.at[stage, at(place)],
                send_sem=send_sems.at[stage, offset],
                recv_sem=land_sems.at[stage, offset],
                device_id={"gx": peer},
                device_id_type=MESH,
            )
            copy.start()
            copies.append(copy)
        lands[stage, at(place), :] = sends[stage, at(place), :]
        return copies

    def finish(copies):
        for copy in copies:
            copy.wait()

    def build_z(z, carry):
        row = z_ref[pl.ds(z, 1), :]
        high = row.astype(jnp.bfloat16).astype(jnp.float32)
        low = row - high
        lane = lax.broadcasted_iota(jnp.int32, (CH, 2 * mode_width), 1)
        keep = lane % CH == lax.broadcasted_iota(jnp.int32, (CH, 2 * mode_width), 0)
        rows = pl.ds(pl.multiple_of(z * CH, CH), CH)
        z_high[rows, :] = jnp.where(keep, high, 0.0).astype(jnp.bfloat16)
        z_low[rows, :] = jnp.where(keep, low, 0.0).astype(jnp.bfloat16)
        return carry

    lax.fori_loop(0, NZ, build_z, 0)
    data_high, data_low = split_bf16(body_ref[...].reshape(cells_x * cells_y, merged_width))
    for ri in range(2):
        columns = slice(ri * mode_width, (ri + 1) * mode_width)
        part = jnp.dot(data_high, z_high[:, columns], preferred_element_type=jnp.float32)
        part += jnp.dot(data_high, z_low[:, columns], preferred_element_type=jnp.float32)
        part += jnp.dot(data_low, z_high[:, columns], preferred_element_type=jnp.float32)
        for x in range(cells_x):
            rows = pl.ds(x * 2 + ri, cells_y, stride=2 * cells_x)
            for q in range(mode_width // 128):
                lanes = slice(q * 128, (q + 1) * 128)
                spectrum[q, rows, :] = part[x * cells_y : (x + 1) * cells_y, lanes]
    for q in range(mode_width // 128):
        sends[0, :, q * 128 : (q + 1) * 128] = spectrum[q]

    pl.semaphore_wait(barrier, count - 1)
    copies = exchange(0)

    up = pltpu.make_async_remote_copy(
        src_ref=body_ref.at[pl.ds(cells_x - 2, 2)], dst_ref=below, send_sem=halo_send.at[0],
        recv_sem=halo_land.at[0], device_id={"gx": lax.rem(place + 1, count)}, device_id_type=MESH,
    )
    down = pltpu.make_async_remote_copy(
        src_ref=body_ref.at[pl.ds(0, 2)], dst_ref=above, send_sem=halo_send.at[1],
        recv_sem=halo_land.at[1], device_id={"gx": lax.rem(place + last, count)}, device_id_type=MESH,
    )

    lane_block = lax.broadcasted_iota(jnp.int32, (CH, LANES), 1) // CH

    def build_weights(tap_ref):
        def per_shift(dx, carry):
            zero = jnp.zeros((CH, LANES), jnp.float32)

            def put(row, value):
                high, low = split_bf16(value)
                b_high[dx, row : row + CH, :] = high
                b_low[dx, row : row + CH, :] = low

            for dy in range(3):
                taps = [
                    jnp.concatenate([tap_ref[dx * 9 + dy * 3 + e]] * STEP, axis=1) for e in range(3)
                ]
                for i in range(STEP):
                    row = zero
                    for e in range(3):
                        row = jnp.where(lane_block == i + 1 - e, taps[e], row)
                    put(dy * LANES + i * CH, row)
                following = jnp.where(lane_block == STEP - 1, taps[2], 0.0)
                previous = jnp.where(lane_block == 0, taps[0], 0.0)
                offsets = ((0, 96), (64, 32), (128, 224))[dy]
                put(3 * LANES + offsets[0], following)
                put(3 * LANES + offsets[1], previous)
            put(3 * LANES + 160, zero)
            put(3 * LANES + 192, zero)
            return carry

        lax.fori_loop(0, 3, per_shift, 0)

    row_y = lax.broadcasted_iota(jnp.int32, (cells_y, 128), 0)
    lane = lax.broadcasted_iota(jnp.int32, (cells_y, 128), 1)
    row_wide = lax.broadcasted_iota(jnp.int32, (cells_y, LANES), 0)

    def shifted(value, dy, rows):
        if dy == 1:
            return value
        if dy == 0:
            return jnp.where(rows == 0, 0.0, pltpu.roll(value, 1, 0))
        return jnp.where(rows == cells_y - 1, 0.0, pltpu.roll(value, cells_y - 1, 0))

    def build_plane(slot, fetch):
        for b in range(BLOCKS):
            rows = slice(b * cells_y, (b + 1) * cells_y)

            def put(column, value):
                high, low = split_bf16(value)
                width = value.shape[1]
                a_high[slot, rows, column : column + width] = high
                a_low[slot, rows, column : column + width] = low

            main = fetch(b * LANES, LANES)
            edge = jnp.zeros((cells_y, 128), jnp.float32)
            if b > 0:
                edge = jnp.where(lane >= 96, fetch(b * LANES - 128, 128), edge)
            if b < BLOCKS - 1:
                edge = jnp.where(lane < CH, fetch((b + 1) * LANES, 128), edge)
            for dy in range(3):
                put(dy * LANES, shifted(main, dy, row_wide))
            put(3 * LANES, shifted(edge, 0, row_y) + pltpu.roll(edge, 64, 1))
            put(3 * LANES + 128, shifted(edge, 2, row_y))

    def multiply(plane):
        total = jnp.zeros((BLOCKS * cells_y, LANES), jnp.float32)
        for dx in range(3):
            left_high = a_high[plane + dx]
            left_low = a_low[plane + dx]
            right_high = b_high[dx]
            total += jnp.dot(left_high, right_high, preferred_element_type=jnp.float32)
            total += jnp.dot(left_high, b_low[dx], preferred_element_type=jnp.float32)
            total += jnp.dot(left_low, right_high, preferred_element_type=jnp.float32)
        return total

    def from_ref(ref, x):
        return lambda column, width: ref[x, :, column : column + width]

    def inner(x, carry):
        build_plane(x + 2, from_ref(body_ref, x))
        return carry

    def lower(x, carry):
        build_plane(x, from_ref(below, x))
        return carry

    def upper(x, carry):
        build_plane(cells_x + 2 + x, from_ref(above, x))
        return carry

    lax.fori_loop(0, chunks // 2, pack, 0)

    finish(copies)
    sends[1] = jnp.dot(x_in_ref[...], lands[0], precision=HIGHEST, preferred_element_type=jnp.float32)
    copies = exchange(1)

    lax.fori_loop(chunks // 2, chunks, pack, 0)

    finish(copies)
    @pl.when(place < last)
    def _():
        up.start()

    @pl.when(place > 0)
    def _():
        down.start()

    modes = jnp.dot(y_in_ref[...], lands[1], precision=HIGHEST, preferred_element_type=jnp.float32)
    for q in range(quarter):
        spectrum[q] = modes[:, q * 128 : (q + 1) * 128]
    height = 2 * pairs

    def mix(step, total):
        rows = []
        for q in range(quarter):
            real, imag = spectrum[q, :pairs], spectrum[q, pairs:]
            columns = []
            for half in range(2):
                lines = pl.ds(pl.multiple_of((2 * step + half) * pairs, pairs), pairs)
                weight_real, weight_imag = packed[q, 0, lines, :], packed[q, 1, lines, :]
                columns.append(
                    jnp.concatenate(
                        [real * weight_real - imag * weight_imag, real * weight_imag + imag * weight_real],
                        axis=0,
                    )
                )
            rows.append(jnp.concatenate(columns, axis=1))
        high, low = split_bf16(jnp.concatenate(rows, axis=0))
        source = lax.broadcasted_iota(jnp.int32, (256, 128), 0)
        target = lax.broadcasted_iota(jnp.int32, (256, 128), 1)
        place_of = (source % 128) // CH * CH + 2 * step + source // 128
        gather = jnp.where(place_of == target, 1.0, 0.0).astype(jnp.bfloat16)
        total += jnp.dot(high, gather, preferred_element_type=jnp.float32)
        return total + jnp.dot(low, gather, preferred_element_type=jnp.float32)

    mixed = lax.fori_loop(0, CH // 2, mix, jnp.zeros((quarter * height, 128), jnp.float32))
    for q in range(quarter):
        sends[2, :, q * 128 : (q + 1) * 128] = jnp.dot(
            y_out_ref[...], mixed[q * height : (q + 1) * height],
            precision=HIGHEST, preferred_element_type=jnp.float32,
        )
    copies = exchange(2)

    build_weights(first_ref)
    lax.fori_loop(0, cells_x, inner, 0)

    @pl.when(place < last)
    def _():
        up.wait_send()
        down.wait_recv()

    @pl.when(place == last)
    def _():
        above[...] = jnp.zeros_like(above)

    @pl.when(place > 0)
    def _():
        down.wait_send()
        up.wait_recv()

    @pl.when(place == 0)
    def _():
        below[...] = jnp.zeros_like(below)

    lax.fori_loop(0, 2, lower, 0)
    lax.fori_loop(0, 2, upper, 0)

    def first(plane, carry):
        inside = jnp.logical_and(
            jnp.logical_or(plane > 0, place > 0),
            jnp.logical_or(plane < cells_x + 1, place < last),
        )
        hidden[plane] = jnp.where(inside, gelu(multiply(plane)), 0.0)
        return carry

    lax.fori_loop(0, cells_x + 2, first, 0)

    finish(copies)
    sends[3] = jnp.dot(x_out_ref[...], lands[2], precision=HIGHEST, preferred_element_type=jnp.float32)
    copies = exchange(3)

    build_weights(second_ref)

    def rebuild(plane, carry):
        def fetch(column, width):
            b = column // LANES
            start = column - b * LANES
            return hidden[plane, b * cells_y : (b + 1) * cells_y, start : start + width]

        build_plane(plane, fetch)
        return carry

    lax.fori_loop(0, cells_x + 2, rebuild, 0)

    def second(plane, carry):
        total = multiply(plane)
        for b in range(BLOCKS):
            out_ref[plane, :, b * LANES : (b + 1) * LANES] = (
                total[b * cells_y : (b + 1) * cells_y] + bias_ref[...]
            )
        return carry

    lax.fori_loop(0, cells_x, second, 0)

    finish(copies)
    for q in range(mode_width // 128):
        spectrum[q] = lands[3, :, q * 128 : (q + 1) * 128]
    lines = []
    for x in range(cells_x):
        lines.append(
            jnp.concatenate(
                [
                    spectrum[q, pl.ds(x * 2 + ri, cells_y, stride=2 * cells_x), :]
                    for ri in range(2)
                    for q in range(mode_width // 128)
                ],
                axis=1,
            )
        )
    line_high, line_low = split_bf16(jnp.concatenate(lines, axis=0) * scale_ref[...])
    across = (((1,), (1,)), ((), ()))
    for b in range(BLOCKS):
        rows = slice(b * LANES, (b + 1) * LANES)
        part = lax.dot_general(line_high, z_high[rows, :], across, preferred_element_type=jnp.float32)
        part += lax.dot_general(line_high, z_low[rows, :], across, preferred_element_type=jnp.float32)
        part += lax.dot_general(line_low, z_high[rows, :], across, preferred_element_type=jnp.float32)
        for x in range(cells_x):
            out_ref[x, :, rows] = gelu(out_ref[x, :, rows] + part[x * cells_y : (x + 1) * cells_y])


def kept_list(length, retained):
    spots = np.arange(retained)
    return np.where(spots < retained // 2, spots, length - retained + spots)


def rotation(angle_index, length, inverse):
    angle = angle_index % length * (2.0 * math.pi / length)
    cos, sin = np.cos(angle), np.sin(angle)
    sign = -1.0 if inverse else 1.0
    return np.stack([np.stack([cos, sign * sin], -1), np.stack([-sign * sin, cos], -1)], -2)


def tables(cells_x, cells_y, count):
    extent_x, owned_x, rows_y = cells_x * count, MX // count, cells_y // count
    x_turn = rotation(kept_list(extent_x, MX)[:, None] * np.arange(extent_x)[None], extent_x, False)
    y_turn = rotation(kept_list(cells_y, MY)[:, None] * np.arange(cells_y)[None], cells_y, False)
    x_turn = x_turn.reshape(count, owned_x, count, cells_x, 2, 2)
    y_turn = y_turn.reshape(MY, count, rows_y, 2, 2)
    same_y, same_x = np.eye(rows_y), np.eye(owned_x)
    x_in = np.einsum("ekdxab,yw->ekyadwxb", x_turn, same_y).reshape(count * owned_x * rows_y * 2, -1)
    y_in = np.einsum("ldyab,kj->alkdjyb", y_turn, same_x).reshape(MY * owned_x * 2, -1)
    y_out = np.einsum("leyba,kj->eykablj", y_turn, same_x).reshape(count * rows_y * owned_x * 2, -1)
    x_out = np.einsum("dkexba,yw->eyxadwkb", x_turn, same_y).reshape(count * rows_y * cells_x * 2, -1)
    angle = np.arange(NZ)[:, None] * np.arange(MZ)[None] % NZ * (2.0 * math.pi / NZ)
    z_table = np.repeat(np.stack([np.cos(angle), -np.sin(angle)], 1).reshape(NZ, 2 * MZ), CH, axis=1)
    scale = np.where(np.arange(MZ) == 0, 1.0, 2.0) / (extent_x * cells_y * NZ)
    scale = np.repeat(np.tile(scale, 2), CH)[None]
    return [jnp.asarray(t, jnp.float32) for t in (z_table, scale, x_in, y_in, y_out, x_out)]


def line_body(field, spectral, conv_first, conv_second, bias):
    cells_x, cells_y, merged_width = field.shape
    count = lax.axis_size("gx")
    mode_width = MZ * CH
    total_rows = cells_x * cells_y * 2
    rows = BLOCKS * cells_y
    vmem = pl.BlockSpec(memory_space=pltpu.VMEM)
    quarter = mode_width // 128
    return pl.pallas_call(
        functools.partial(block_kernel, count),
        out_shape=jax.ShapeDtypeStruct(field.shape, jnp.float32),
        in_specs=[vmem, pl.BlockSpec(memory_space=pl.ANY)] + [vmem] * 9,
        out_specs=vmem,
        scratch_shapes=[
            pltpu.VMEM((3, DEPTH, LANES), jnp.bfloat16),
            pltpu.VMEM((3, DEPTH, LANES), jnp.bfloat16),
            pltpu.VMEM((cells_x + 4, rows, DEPTH), jnp.bfloat16),
            pltpu.VMEM((cells_x + 4, rows, DEPTH), jnp.bfloat16),
            pltpu.VMEM((cells_x + 2, rows, LANES), jnp.float32),
            pltpu.VMEM((merged_width, 2 * mode_width), jnp.bfloat16),
            pltpu.VMEM((merged_width, 2 * mode_width), jnp.bfloat16),
            pltpu.VMEM((4, 2) + spectral.shape[1:], jnp.float32),
            pltpu.VMEM((quarter, 2, CH * MY * spectral.shape[1], 128), jnp.float32),
            pltpu.VMEM((quarter, total_rows, 128), jnp.float32),
            pltpu.VMEM((2, cells_y, merged_width), jnp.float32),
            pltpu.VMEM((2, cells_y, merged_width), jnp.float32),
            pltpu.VMEM((4, total_rows, mode_width), jnp.float32),
            pltpu.VMEM((4, total_rows, mode_width), jnp.float32),
            pltpu.SemaphoreType.DMA((4, count)),
            pltpu.SemaphoreType.DMA((4, count)),
            pltpu.SemaphoreType.DMA((2,)),
            pltpu.SemaphoreType.DMA((2,)),
            pltpu.SemaphoreType.DMA((4,)),
        ],
        compiler_params=pltpu.CompilerParams(
            collective_id=0, has_side_effects=True, vmem_limit_bytes=63 * 2**20
        ),
    )(
        field, spectral, conv_first.reshape(27, CH, CH), conv_second.reshape(27, CH, CH),
        jnp.tile(bias, STEP)[None], *tables(cells_x, cells_y, count),
    )


def solution(mesh):
    in_specs = (
        P(("groups", "gx"), "gy", None),
        P("gy", "gx", None, None, None, None),
        P(),
        P(),
        P(),
    )
    out_specs = P(("groups", "gx"), "gy", None)
    count = mesh.shape["gx"]

    def chosen(field, *rest):
        whole = (field.shape[0] * count, field.shape[1] * mesh.shape["gy"])
        fits = whole == (MX, MY) and mesh.shape["gy"] == 1 and MX == MY == 2 * count
        return (line_body if fits else body)(field, *rest)

    return jax.shard_map(chosen, mesh=mesh, in_specs=in_specs, out_specs=out_specs, check_vma=False)
```

```python
import functools
import math

import jax
import jax.numpy as jnp
import numpy as np
from jax import lax
from jax.experimental import pallas as pl
from jax.experimental.pallas import tpu as pltpu
from jax.sharding import PartitionSpec as P

CH = 32
NZ = 64
MX = 32
MY = 32
MZ = 16


HIGHEST = lax.Precision.HIGHEST
HIGH = lax.Precision.HIGH


def with_halo(cells, sides, width):
    for axis, dim in sides:
        count = lax.axis_size(axis)
        ends = count - 1
        head = lax.slice_in_dim(cells, 0, width, axis=dim)
        tail = lax.slice_in_dim(cells, cells.shape[dim] - width, cells.shape[dim], axis=dim)
        cells = jnp.concatenate(
            [
                lax.ppermute(tail, axis, [(i, (i + 1) % count) for i in range(ends)]),
                cells,
                lax.ppermute(head, axis, [((i + 1) % count, i) for i in range(ends)]),
            ],
            axis=dim,
        )
    return cells


def frequency(position, length, retained):
    return jnp.where(position < retained // 2, position, length - retained + position)


def angle_table(first_list, second_list, length):
    product = first_list[:, None] * second_list[None, :] % length
    angles = product.astype(jnp.float32) * (2.0 * math.pi / length)
    return (jnp.cos(angles), jnp.sin(angles))


def rotate_sum(cos_table, sin_table, values, pattern, direction_sign):
    real_part = values[:, :, 0]
    imag_part = values[:, :, 1]
    out_real = jnp.einsum(
        pattern, cos_table, real_part, precision=HIGHEST
    ) + direction_sign * jnp.einsum(pattern, sin_table, imag_part, precision=HIGHEST)
    out_imag = jnp.einsum(
        pattern, cos_table, imag_part, precision=HIGHEST
    ) - direction_sign * jnp.einsum(pattern, sin_table, real_part, precision=HIGHEST)
    return jnp.stack([out_real, out_imag], axis=2)


def convolve(padded, weight):
    extent_x = padded.shape[0] - 2
    extent_y = padded.shape[1] - 2
    volume = padded.reshape(padded.shape[0], padded.shape[1], NZ, CH)
    volume = jnp.pad(volume, ((0, 0), (0, 0), (1, 1), (0, 0)))
    kernel = weight.reshape(3, 3, 3 * CH, CH)

    def plane(start):
        slab = lax.dynamic_slice_in_dim(volume, start, 3, 0)
        accumulated = jnp.zeros((extent_y, NZ, CH), jnp.float32)
        for shift_x in range(3):
            for shift_y in range(3):
                windowed = slab[shift_x, shift_y : shift_y + extent_y]
                stacked = jnp.concatenate(
                    [windowed[:, shift_z : shift_z + NZ] for shift_z in range(3)], axis=2
                )
                accumulated = accumulated + jnp.einsum(
                    "yzi,io->yzo", stacked, kernel[shift_x, shift_y], precision=HIGHEST
                )
        return accumulated

    return lax.map(plane, jnp.arange(extent_x, dtype=jnp.int32))


def mode_mix(inputs, matrix):
    return jnp.einsum("bazi,bazio->bazo", inputs, matrix, precision=HIGHEST)


def body(field, spectral, conv_first, conv_second, bias):
    cells_x, cells_y, merged_width = field.shape
    devices_x = lax.axis_size("gx")
    devices_y = lax.axis_size("gy")
    extent_x = cells_x * devices_x
    extent_y = cells_y * devices_y
    owned_x = MX // devices_x
    owned_y = MY // devices_y
    y_places = lax.axis_index("gy") * cells_y + jnp.arange(cells_y, dtype=jnp.int32)
    mode_width = MZ * CH
    volume = field.reshape(cells_x, cells_y, NZ, CH)
    z_modes_index = jnp.arange(MZ, dtype=jnp.int32)
    z_cos, z_sin = angle_table(z_modes_index, jnp.arange(NZ, dtype=jnp.int32), NZ)
    z_real = jnp.einsum("xyzc,kz->xykc", volume, z_cos, precision=HIGHEST)
    z_imag = -jnp.einsum("xyzc,kz->xykc", volume, z_sin, precision=HIGHEST)
    z_spectrum = jnp.stack([z_real, z_imag], axis=2).reshape(cells_x, cells_y, 2, mode_width)
    cos_table, sin_table = angle_table(
        frequency(jnp.arange(MX, dtype=jnp.int32), extent_x, MX),
        jnp.arange(extent_x, dtype=jnp.int32),
        extent_x,
    )
    kept_modes = rotate_sum(
        cos_table,
        sin_table,
        lax.all_to_all(z_spectrum, "gx", split_axis=1, concat_axis=0, tiled=True),
        "kx,xym->kym",
        1.0,
    )
    x_modes = lax.all_to_all(kept_modes, "gx", split_axis=0, concat_axis=1, tiled=True)
    row_index = jnp.arange(owned_y * lax.axis_size("gy"), dtype=jnp.int32)
    cos_table, sin_table = angle_table(frequency(row_index, extent_y, MY), y_places, extent_y)
    all_modes = lax.psum_scatter(
        rotate_sum(cos_table, sin_table, x_modes, "ky,xym->kxm", 1.0),
        "gy",
        scatter_dimension=0,
        tiled=True,
    )
    complex_parts = all_modes.reshape(owned_y, owned_x, 2, MZ, CH)
    real_inputs = complex_parts[:, :, 0]
    imag_inputs = complex_parts[:, :, 1]
    weight_real = spectral[:, :, :, 0]
    weight_imag = spectral[:, :, :, 1]
    mixed_real = mode_mix(real_inputs, weight_real) - mode_mix(imag_inputs, weight_imag)
    mixed_imag = mode_mix(real_inputs, weight_imag) + mode_mix(imag_inputs, weight_real)
    mixed = jnp.stack([mixed_real, mixed_imag], axis=2).reshape(owned_y, owned_x, 2, mode_width)
    portion = lax.all_gather(mixed, "gy", axis=0, tiled=True)
    row_index = jnp.arange(portion.shape[0], dtype=jnp.int32)
    cos_table, sin_table = angle_table(y_places, frequency(row_index, extent_y, MY), extent_y)
    y_cells = rotate_sum(cos_table, sin_table, portion, "yk,kxm->xym", -1.0)
    cos_table, sin_table = angle_table(
        jnp.arange(extent_x, dtype=jnp.int32),
        frequency(jnp.arange(MX, dtype=jnp.int32), extent_x, MX),
        extent_x,
    )
    cell_lines = rotate_sum(
        cos_table,
        sin_table,
        lax.all_to_all(y_cells, "gx", split_axis=1, concat_axis=0, tiled=True),
        "xk,kym->xym",
        -1.0,
    )
    planes = lax.all_to_all(cell_lines, "gx", split_axis=0, concat_axis=1, tiled=True)
    z_weights = jnp.where(z_modes_index == 0, 1.0, 2.0).astype(jnp.float32) / (
        extent_x * extent_y * NZ
    )
    planes_split = planes.reshape(cells_x, cells_y, 2, MZ, CH)
    spectral_part = jnp.einsum(
        "xykc,kz->xyzc", planes_split[:, :, 0], z_cos * z_weights[:, None], precision=HIGHEST
    ) - jnp.einsum(
        "xykc,kz->xyzc", planes_split[:, :, 1], z_sin * z_weights[:, None], precision=HIGHEST
    )
    with_rim = with_halo(field, (("gx", 0), ("gy", 1)), 1)
    first_hidden = jax.nn.gelu(convolve(with_rim, conv_first), approximate=False).reshape(
        cells_x, cells_y, merged_width
    )
    hidden_block = with_halo(first_hidden, (("gx", 0), ("gy", 1)), 1)
    second_branch = convolve(hidden_block, conv_second)
    result = jax.nn.gelu(spectral_part + second_branch + bias, approximate=False)
    return result.reshape(cells_x, cells_y, merged_width)


LANES = 256
STEP = LANES // CH
BLOCKS = NZ // STEP
DEPTH = 4 * LANES


def split_bf16(value):
    high = value.astype(jnp.bfloat16)
    low = (value - high.astype(jnp.float32)).astype(jnp.bfloat16)
    return high, low


def erf(value):
    value = jnp.clip(value, -3.832506856900711, 3.832506856900711)
    square = value * value
    top = jnp.float32(0.00022905065861350646)
    for term in (0.0034082910107109506, 0.050955695062380861, 0.18520832239976145, 1.128379143519084):
        top = top * square + term
    bottom = jnp.float32(-1.1791602954361697e-7)
    for term in (0.000023547966471313185, 0.0010179625278914885, 0.014070470171167667, 0.11098505178285362, 0.49746925110067538, 1.0):
        bottom = bottom * square + term
    return value * top / bottom


def gelu(value):
    return value * (1.0 + erf(value * (0.5**0.5))) * 0.5


MESH = pl.DeviceIdType.MESH


def block_kernel(
    count, body_ref, spectral_ref, first_ref, second_ref, bias_ref, z_ref, scale_ref,
    x_in_ref, y_in_ref, y_out_ref, x_out_ref, out_ref,
    b_high, b_low, a_high, a_low, hidden, z_high, z_low, slots, packed, spectrum,
    below, above, sends, lands, send_sems, land_sems, halo_send, halo_land, weight_sem,
):
    cells_x, cells_y, merged_width = body_ref.shape
    owned_x = spectral_ref.shape[1]
    mode_width = MZ * CH
    block = sends.shape[1] // count
    place = lax.axis_index("gx")
    last = count - 1

    barrier = pltpu.get_barrier_semaphore()
    for offset in range(1, count):
        pl.semaphore_signal(
            barrier, inc=1, device_id={"gx": lax.rem(place + offset, count)}, device_id_type=MESH
        )
    slot_count, per_slot = slots.shape[:2]
    chunks = MY // per_slot
    pairs = MY * owned_x
    quarter = mode_width // 128

    def weight_copy(chunk):
        slot = lax.rem(chunk, slot_count)
        return pltpu.make_async_copy(
            spectral_ref.at[pl.ds(chunk * per_slot, per_slot)], slots.at[slot], weight_sem.at[slot]
        )

    for chunk in range(slot_count):
        weight_copy(chunk).start()

    def pack(chunk, carry):
        weight_copy(chunk).wait()
        slot = lax.rem(chunk, slot_count)
        for y in range(per_slot):
            for x in range(owned_x):
                pair = (chunk * per_slot + y) * owned_x + x
                for q in range(quarter):
                    for ri in range(2):
                        tile = jnp.concatenate([slots[slot, y, x, q * 4 + k, ri] for k in range(4)], axis=0)
                        packed[q, ri, pl.ds(pair, CH, stride=pairs), :] = tile.T

        @pl.when(chunk + slot_count < chunks)
        def _():
            weight_copy(chunk + slot_count).start()

        return carry

    def at(index):
        return pl.ds(pl.multiple_of(index * block, 8), block)

    def exchange(stage):
        copies = []
        for offset in [o for k in range(count // 2, 0, -1) for o in sorted({k, count - k})]:
            peer = lax.rem(place + offset, count)
            copy = pltpu.make_async_remote_copy(
                src_ref=sends.at[stage, at(peer)],
                dst_ref=lands.at[stage, at(place)],
                send_sem=send_sems.at[stage, offset],
                recv_sem=land_sems.at[stage, offset],
                device_id={"gx": peer},
                device_id_type=MESH,
            )
            copy.start()
            copies.append(copy)
        lands[stage, at(place), :] = sends[stage, at(place), :]
        return copies

    def finish(copies):
        for copy in copies:
            copy.wait()

    def build_z(z, carry):
        row = z_ref[pl.ds(z, 1), :]
        high = row.astype(jnp.bfloat16).astype(jnp.float32)
        low = row - high
        lane = lax.broadcasted_iota(jnp.int32, (CH, 2 * mode_width), 1)
        keep = lane % CH == lax.broadcasted_iota(jnp.int32, (CH, 2 * mode_width), 0)
        rows = pl.ds(pl.multiple_of(z * CH, CH), CH)
        z_high[rows, :] = jnp.where(keep, high, 0.0).astype(jnp.bfloat16)
        z_low[rows, :] = jnp.where(keep, low, 0.0).astype(jnp.bfloat16)
        return carry

    lax.fori_loop(0, NZ, build_z, 0)
    data_high, data_low = split_bf16(body_ref[...].reshape(cells_x * cells_y, merged_width))
    for ri in range(2):
        columns = slice(ri * mode_width, (ri + 1) * mode_width)
        part = jnp.dot(data_high, z_high[:, columns], preferred_element_type=jnp.float32)
        part += jnp.dot(data_high, z_low[:, columns], preferred_element_type=jnp.float32)
        part += jnp.dot(data_low, z_high[:, columns], preferred_element_type=jnp.float32)
        for x in range(cells_x):
            rows = pl.ds(x * 2 + ri, cells_y, stride=2 * cells_x)
            for q in range(mode_width // 128):
                lanes = slice(q * 128, (q + 1) * 128)
                spectrum[q, rows, :] = part[x * cells_y : (x + 1) * cells_y, lanes]
    for q in range(mode_width // 128):
        sends[0, :, q * 128 : (q + 1) * 128] = spectrum[q]

    pl.semaphore_wait(barrier, count - 1)
    copies = exchange(0)

    up = pltpu.make_async_remote_copy(
        src_ref=body_ref.at[pl.ds(cells_x - 2, 2)], dst_ref=below, send_sem=halo_send.at[0],
        recv_sem=halo_land.at[0], device_id={"gx": lax.rem(place + 1, count)}, device_id_type=MESH,
    )
    down = pltpu.make_async_remote_copy(
        src_ref=body_ref.at[pl.ds(0, 2)], dst_ref=above, send_sem=halo_send.at[1],
        recv_sem=halo_land.at[1], device_id={"gx": lax.rem(place + last, count)}, device_id_type=MESH,
    )

    lane_block = lax.broadcasted_iota(jnp.int32, (CH, LANES), 1) // CH

    def build_weights(tap_ref):
        def per_shift(dx, carry):
            zero = jnp.zeros((CH, LANES), jnp.float32)

            def put(row, value):
                high, low = split_bf16(value)
                b_high[dx, row : row + CH, :] = high
                b_low[dx, row : row + CH, :] = low

            for dy in range(3):
                taps = [
                    jnp.concatenate([tap_ref[dx * 9 + dy * 3 + e]] * STEP, axis=1) for e in range(3)
                ]
                for i in range(STEP):
                    row = zero
                    for e in range(3):
                        row = jnp.where(lane_block == i + 1 - e, taps[e], row)
                    put(dy * LANES + i * CH, row)
                following = jnp.where(lane_block == STEP - 1, taps[2], 0.0)
                previous = jnp.where(lane_block == 0, taps[0], 0.0)
                offsets = ((0, 96), (64, 32), (128, 224))[dy]
                put(3 * LANES + offsets[0], following)
                put(3 * LANES + offsets[1], previous)
            put(3 * LANES + 160, zero)
            put(3 * LANES + 192, zero)
            return carry

        lax.fori_loop(0, 3, per_shift, 0)

    row_y = lax.broadcasted_iota(jnp.int32, (cells_y, 128), 0)
    lane = lax.broadcasted_iota(jnp.int32, (cells_y, 128), 1)
    row_wide = lax.broadcasted_iota(jnp.int32, (cells_y, LANES), 0)

    def shifted(value, dy, rows):
        if dy == 1:
            return value
        if dy == 0:
            return jnp.where(rows == 0, 0.0, pltpu.roll(value, 1, 0))
        return jnp.where(rows == cells_y - 1, 0.0, pltpu.roll(value, cells_y - 1, 0))

    def build_plane(slot, fetch):
        for b in range(BLOCKS):
            rows = slice(b * cells_y, (b + 1) * cells_y)

            def put(column, value):
                high, low = split_bf16(value)
                width = value.shape[1]
                a_high[slot, rows, column : column + width] = high
                a_low[slot, rows, column : column + width] = low

            main = fetch(b * LANES, LANES)
            edge = jnp.zeros((cells_y, 128), jnp.float32)
            if b > 0:
                edge = jnp.where(lane >= 96, fetch(b * LANES - 128, 128), edge)
            if b < BLOCKS - 1:
                edge = jnp.where(lane < CH, fetch((b + 1) * LANES, 128), edge)
            for dy in range(3):
                put(dy * LANES, shifted(main, dy, row_wide))
            put(3 * LANES, shifted(edge, 0, row_y) + pltpu.roll(edge, 64, 1))
            put(3 * LANES + 128, shifted(edge, 2, row_y))

    def multiply(plane):
        total = jnp.zeros((BLOCKS * cells_y, LANES), jnp.float32)
        for dx in range(3):
            left_high = a_high[plane + dx]
            left_low = a_low[plane + dx]
            right_high = b_high[dx]
            total += jnp.dot(left_high, right_high, preferred_element_type=jnp.float32)
            total += jnp.dot(left_high, b_low[dx], preferred_element_type=jnp.float32)
            total += jnp.dot(left_low, right_high, preferred_element_type=jnp.float32)
        return total

    def from_ref(ref, x):
        return lambda column, width: ref[x, :, column : column + width]

    def inner(x, carry):
        build_plane(x + 2, from_ref(body_ref, x))
        return carry

    def lower(x, carry):
        build_plane(x, from_ref(below, x))
        return carry

    def upper(x, carry):
        build_plane(cells_x + 2 + x, from_ref(above, x))
        return carry

    lax.fori_loop(0, chunks // 2, pack, 0)
    build_weights(first_ref)

    finish(copies)
    sends[1] = jnp.dot(x_in_ref[...], lands[0], precision=HIGHEST, preferred_element_type=jnp.float32)
    copies = exchange(1)

    lax.fori_loop(chunks // 2, chunks, pack, 0)
    lax.fori_loop(0, cells_x, inner, 0)

    finish(copies)
    @pl.when(place < last)
    def _():
        up.start()

    @pl.when(place > 0)
    def _():
        down.start()

    modes = jnp.dot(y_in_ref[...], lands[1], precision=HIGHEST, preferred_element_type=jnp.float32)
    for q in range(quarter):
        spectrum[q] = modes[:, q * 128 : (q + 1) * 128]
    height = 2 * pairs

    def mix(step, total):
        rows = []
        for q in range(quarter):
            real, imag = spectrum[q, :pairs], spectrum[q, pairs:]
            columns = []
            for half in range(2):
                lines = pl.ds(pl.multiple_of((2 * step + half) * pairs, pairs), pairs)
                weight_real, weight_imag = packed[q, 0, lines, :], packed[q, 1, lines, :]
                columns.append(
                    jnp.concatenate(
                        [real * weight_real - imag * weight_imag, real * weight_imag + imag * weight_real],
                        axis=0,
                    )
                )
            rows.append(jnp.concatenate(columns, axis=1))
        high, low = split_bf16(jnp.concatenate(rows, axis=0))
        source = lax.broadcasted_iota(jnp.int32, (256, 128), 0)
        target = lax.broadcasted_iota(jnp.int32, (256, 128), 1)
        place_of = (source % 128) // CH * CH + 2 * step + source // 128
        gather = jnp.where(place_of == target, 1.0, 0.0).astype(jnp.bfloat16)
        total += jnp.dot(high, gather, preferred_element_type=jnp.float32)
        return total + jnp.dot(low, gather, preferred_element_type=jnp.float32)

    mixed = lax.fori_loop(0, CH // 2, mix, jnp.zeros((quarter * height, 128), jnp.float32))
    for q in range(quarter):
        sends[2, :, q * 128 : (q + 1) * 128] = jnp.dot(
            y_out_ref[...], mixed[q * height : (q + 1) * height],
            precision=HIGHEST, preferred_element_type=jnp.float32,
        )
    copies = exchange(2)


    @pl.when(place < last)
    def _():
        up.wait_send()
        down.wait_recv()

    @pl.when(place == last)
    def _():
        above[...] = jnp.zeros_like(above)

    @pl.when(place > 0)
    def _():
        down.wait_send()
        up.wait_recv()

    @pl.when(place == 0)
    def _():
        below[...] = jnp.zeros_like(below)

    lax.fori_loop(0, 2, lower, 0)
    lax.fori_loop(0, 2, upper, 0)

    def first(plane, carry):
        inside = jnp.logical_and(
            jnp.logical_or(plane > 0, place > 0),
            jnp.logical_or(plane < cells_x + 1, place < last),
        )
        hidden[plane] = jnp.where(inside, gelu(multiply(plane)), 0.0)
        return carry

    lax.fori_loop(0, cells_x + 2, first, 0)

    finish(copies)
    sends[3] = jnp.dot(x_out_ref[...], lands[2], precision=HIGHEST, preferred_element_type=jnp.float32)
    copies = exchange(3)

    build_weights(second_ref)

    def rebuild(plane, carry):
        def fetch(column, width):
            b = column // LANES
            start = column - b * LANES
            return hidden[plane, b * cells_y : (b + 1) * cells_y, start : start + width]

        build_plane(plane, fetch)
        return carry

    lax.fori_loop(0, cells_x + 2, rebuild, 0)

    shift = jnp.concatenate([bias_ref[...]] * STEP, axis=1)

    def second(plane, carry):
        total = multiply(plane)
        for b in range(BLOCKS):
            out_ref[plane, :, b * LANES : (b + 1) * LANES] = (
                total[b * cells_y : (b + 1) * cells_y] + shift
            )
        return carry

    lax.fori_loop(0, cells_x, second, 0)

    finish(copies)
    for q in range(mode_width // 128):
        spectrum[q] = lands[3, :, q * 128 : (q + 1) * 128]
    lines = []
    for x in range(cells_x):
        lines.append(
            jnp.concatenate(
                [
                    spectrum[q, pl.ds(x * 2 + ri, cells_y, stride=2 * cells_x), :]
                    for ri in range(2)
                    for q in range(mode_width // 128)
                ],
                axis=1,
            )
        )
    line_high, line_low = split_bf16(jnp.concatenate(lines, axis=0) * scale_ref[...])
    across = (((1,), (1,)), ((), ()))
    for b in range(BLOCKS):
        rows = slice(b * LANES, (b + 1) * LANES)
        part = lax.dot_general(line_high, z_high[rows, :], across, preferred_element_type=jnp.float32)
        part += lax.dot_general(line_high, z_low[rows, :], across, preferred_element_type=jnp.float32)
        part += lax.dot_general(line_low, z_high[rows, :], across, preferred_element_type=jnp.float32)
        for x in range(cells_x):
            out_ref[x, :, rows] = gelu(out_ref[x, :, rows] + part[x * cells_y : (x + 1) * cells_y])


def kept_list(length, retained):
    spots = np.arange(retained)
    return np.where(spots < retained // 2, spots, length - retained + spots)


def rotation(angle_index, length, inverse):
    angle = angle_index % length * (2.0 * math.pi / length)
    cos, sin = np.cos(angle), np.sin(angle)
    sign = -1.0 if inverse else 1.0
    return np.stack([np.stack([cos, sign * sin], -1), np.stack([-sign * sin, cos], -1)], -2)


def tables(cells_x, cells_y, count):
    extent_x, owned_x, rows_y = cells_x * count, MX // count, cells_y // count
    x_turn = rotation(kept_list(extent_x, MX)[:, None] * np.arange(extent_x)[None], extent_x, False)
    y_turn = rotation(kept_list(cells_y, MY)[:, None] * np.arange(cells_y)[None], cells_y, False)
    x_turn = x_turn.reshape(count, owned_x, count, cells_x, 2, 2)
    y_turn = y_turn.reshape(MY, count, rows_y, 2, 2)
    same_y, same_x = np.eye(rows_y), np.eye(owned_x)
    x_in = np.einsum("ekdxab,yw->ekyadwxb", x_turn, same_y).reshape(count * owned_x * rows_y * 2, -1)
    y_in = np.einsum("ldyab,kj->alkdjyb", y_turn, same_x).reshape(MY * owned_x * 2, -1)
    y_out = np.einsum("leyba,kj->eykablj", y_turn, same_x).reshape(count * rows_y * owned_x * 2, -1)
    x_out = np.einsum("dkexba,yw->eyxadwkb", x_turn, same_y).reshape(count * rows_y * cells_x * 2, -1)
    angle = np.arange(NZ)[:, None] * np.arange(MZ)[None] % NZ * (2.0 * math.pi / NZ)
    z_table = np.repeat(np.stack([np.cos(angle), -np.sin(angle)], 1).reshape(NZ, 2 * MZ), CH, axis=1)
    scale = np.where(np.arange(MZ) == 0, 1.0, 2.0) / (extent_x * cells_y * NZ)
    scale = np.repeat(np.tile(scale, 2), CH)[None]
    return [jnp.asarray(t, jnp.float32) for t in (z_table, scale, x_in, y_in, y_out, x_out)]


def line_body(field, spectral, conv_first, conv_second, bias):
    cells_x, cells_y, merged_width = field.shape
    count = lax.axis_size("gx")
    mode_width = MZ * CH
    total_rows = cells_x * cells_y * 2
    rows = BLOCKS * cells_y
    vmem = pl.BlockSpec(memory_space=pltpu.VMEM)
    quarter = mode_width // 128
    return pl.pallas_call(
        functools.partial(block_kernel, count),
        out_shape=jax.ShapeDtypeStruct(field.shape, jnp.float32),
        in_specs=[vmem, pl.BlockSpec(memory_space=pl.ANY)] + [vmem] * 9,
        out_specs=vmem,
        scratch_shapes=[
            pltpu.VMEM((3, DEPTH, LANES), jnp.bfloat16),
            pltpu.VMEM((3, DEPTH, LANES), jnp.bfloat16),
            pltpu.VMEM((cells_x + 4, rows, DEPTH), jnp.bfloat16),
            pltpu.VMEM((cells_x + 4, rows, DEPTH), jnp.bfloat16),
            pltpu.VMEM((cells_x + 2, rows, LANES), jnp.float32),
            pltpu.VMEM((merged_width, 2 * mode_width), jnp.bfloat16),
            pltpu.VMEM((merged_width, 2 * mode_width), jnp.bfloat16),
            pltpu.VMEM((4, 2) + spectral.shape[1:], jnp.float32),
            pltpu.VMEM((quarter, 2, CH * MY * spectral.shape[1], 128), jnp.float32),
            pltpu.VMEM((quarter, total_rows, 128), jnp.float32),
            pltpu.VMEM((2, cells_y, merged_width), jnp.float32),
            pltpu.VMEM((2, cells_y, merged_width), jnp.float32),
            pltpu.VMEM((4, total_rows, mode_width), jnp.float32),
            pltpu.VMEM((4, total_rows, mode_width), jnp.float32),
            pltpu.SemaphoreType.DMA((4, count)),
            pltpu.SemaphoreType.DMA((4, count)),
            pltpu.SemaphoreType.DMA((2,)),
            pltpu.SemaphoreType.DMA((2,)),
            pltpu.SemaphoreType.DMA((4,)),
        ],
        compiler_params=pltpu.CompilerParams(
            collective_id=0, has_side_effects=True, vmem_limit_bytes=63 * 2**20
        ),
    )(
        field, spectral, conv_first.reshape(27, CH, CH), conv_second.reshape(27, CH, CH),
        bias[None], *tables(cells_x, cells_y, count),
    )


def solution(mesh):
    in_specs = (
        P(("groups", "gx"), "gy", None),
        P("gy", "gx", None, None, None, None),
        P(),
        P(),
        P(),
    )
    out_specs = P(("groups", "gx"), "gy", None)
    count = mesh.shape["gx"]

    def chosen(field, *rest):
        whole = (field.shape[0] * count, field.shape[1] * mesh.shape["gy"])
        fits = whole == (MX, MY) and mesh.shape["gy"] == 1 and MX == MY == 2 * count
        return (line_body if fits else body)(field, *rest)

    return jax.shard_map(chosen, mesh=mesh, in_specs=in_specs, out_specs=out_specs, check_vma=False)
```
